32 devices in a mesh: groups: 2 (over y), dp: 4 (over z), tensor: 2 (over x), layer: 2 (over core).
Axes of the slice: x: 2, y: 2, z: 4, core: 2. Of those that a mesh axis runs over, the one named last changes fastest.
Arguments:
- train_inputs: bfloat16 [2, 256, 16, 8192], P('layer', ('groups', 'dp'), None, 'tensor'), parts along dimension 1, may hold values from -6 to 6
- train_grads: bfloat16 [2, 256, 16, 8192], P('layer', ('groups', 'dp'), None, 'tensor'), parts along dimension 1, may hold values from -6 to 6
- bench_inputs: bfloat16 [2, 128, 16, 8192], P('layer', ('groups', 'dp'), None, 'tensor'), parts along dimension 1, may hold values from -6 to 6
- bench_grads: bfloat16 [2, 128, 16, 8192], P('layer', ('groups', 'dp'), None, 'tensor'), parts along dimension 1, may hold values from -6 to 6
- answer_mask: int32 [128, 16], P(('groups', 'dp')), parts along dimension 0, may hold values 0 or 1
- factors: bfloat16 [2, 8192, 128], P('layer', 'tensor'), may hold values from -0.0625 to 0.0625
- precond: bfloat16 [2, 4096, 4096], P('layer', None, ('dp', 'tensor')), may hold values from -0.09375 to 0.09375
Outputs:
- scores: float32 [256, 64], P(('groups', 'dp', 'tensor', 'layer')), parts along dimension 0
The draws below stay inside these ranges and needn't reach their ends.
There are 2 independent parts, one for each index of `groups`. The reference program is written for one: setup_inputs(seed, part) draws one part's arguments, and reference() takes and returns one part's arrays. A program takes and returns all parts, laid end to end along the dimension named above; an argument that names none is the same for every part. Nothing has to cross between parts.
All inputs are finite; a program needn't handle non-finite values. No bound on the sum of `answer_mask` on one device may be relied on, other than what follows from the above.
Results may differ from the reference program's by a relative error of at most 0.005.
Values may be sent and summed in bfloat16 or wider, within the bound.
A program may use at most 64 MiB of HBM per device.

```python
import math
import jax
import jax.numpy as jnp
from jax import lax

D = 8192
K = 64
SEQ = 16
F = 4096
TRAIN = 128
BENCH = 64
LAYERS = 2


def set_ends(entries, rng, smallest, high):
    shape = entries.shape
    index_at = [jax.random.randint(jax.random.fold_in(rng, axis), (), 0, shape[axis]) for axis in range(len(shape))]
    entries = entries.at[tuple(index_at)].set(smallest)
    longest = shape.index(max(shape))
    index_at[longest] = (index_at[longest] + 1) % shape[longest]
    return entries.at[tuple(index_at)].set(high)


def levels(rng, extent, cuts, smallest, largest):
    def one(position, parts):
        draws = jax.random.uniform(jax.random.fold_in(jax.random.fold_in(rng, 6), position), (parts,), jnp.float32, smallest / len(cuts), largest / len(cuts))
        return jnp.repeat(jnp.exp(draws), extent[position] // parts).reshape((-1,) + (1,) * (len(extent) - position - 1))

    loudness = one(*cuts[0])
    for cut in cuts[1:]:
        loudness = loudness * one(*cut)
    return loudness


def normal_values(stream_key, dims, deviation, bound, cuts=(), kind=jnp.bfloat16):
    level = levels(stream_key, dims, cuts, -0.22, 0.18) if cuts else 1.0
    values = jax.random.normal(stream_key, dims, jnp.float32) * deviation * level
    return jnp.minimum(jnp.maximum(values, -bound), bound).astype(kind)


def setup_inputs(seed: int = 0, part: int = 0) -> dict:
    key_list = jax.random.split(jax.random.key(seed), 8)
    part_keys = jax.random.split(jax.random.fold_in(key_list[7], part), 8)
    return {
        "train_inputs": normal_values(part_keys[0], (LAYERS, TRAIN, SEQ, D), 1.0, 6.0, ((0, 2), (1, 4), (3, 2))),
        "train_grads": normal_values(part_keys[1], (LAYERS, TRAIN, SEQ, D), 1.0, 6.0, ((0, 2), (1, 4), (3, 2))),
        "bench_inputs": normal_values(part_keys[2], (LAYERS, BENCH, SEQ, D), 1.0, 6.0, ((0, 2), (1, 4), (3, 2))),
        "bench_grads": normal_values(part_keys[3], (LAYERS, BENCH, SEQ, D), 1.0, 6.0, ((0, 2), (1, 4), (3, 2))),
        "answer_mask": set_ends((jax.random.randint(part_keys[4], (BENCH, SEQ), 0, 2) < 1).astype(jnp.int32), jax.random.fold_in(part_keys[4], 1), 0, 1),
        "factors": normal_values(key_list[5], (LAYERS, D, 2 * K), D ** -0.5, 0.0625, ((0, 2), (1, 2))),
        "precond": normal_values(key_list[6], (LAYERS, F, F), F ** -0.5, 0.09375, ((0, 2), (2, 8))),
    }


def features(inputs_here, grads_here, factor):
    examples = inputs_here.shape[0]
    in_proj = jnp.dot(inputs_here.reshape(examples * SEQ, D), factor[:, :K], preferred_element_type=jnp.float32)
    out_proj = jnp.dot(grads_here.reshape(examples * SEQ, D), factor[:, K:], preferred_element_type=jnp.float32)
    in_proj = in_proj.reshape(examples, SEQ, K)
    out_proj = out_proj.reshape(examples, SEQ, K)
    outer = jnp.einsum('esa,esb->eab', out_proj, in_proj, precision=lax.Precision.HIGHEST) / math.sqrt(SEQ)
    return outer.reshape(examples, K * K).astype(jnp.bfloat16)

def reference(train_inputs, train_grads, bench_inputs, bench_grads, answer_mask, factors, precond):
    total = jnp.zeros((TRAIN, BENCH), jnp.float32)
    mask_values = answer_mask.astype(jnp.bfloat16)[:, :, None]
    for level in range(LAYERS):
        train_feats = features(train_inputs[level], train_grads[level], factors[level])
        bench_feats = features(bench_inputs[level], bench_grads[level] * mask_values, factors[level])
        bench_pre = jnp.dot(bench_feats, precond[level], preferred_element_type=jnp.float32).astype(jnp.bfloat16)
        total = total + jnp.dot(train_feats, bench_pre.T, preferred_element_type=jnp.float32)
    return total / math.sqrt(K * K * LAYERS)
```

```python
import functools
import math

import jax
import jax.numpy as jnp
from jax import lax
from jax.experimental import pallas as pl
from jax.experimental.pallas import tpu as pltpu
from jax.sharding import PartitionSpec as P

MESH = pl.DeviceIdType.MESH


def project(inputs_here, grads_here, factor):
    examples, length, shard_width = inputs_here.shape
    factor_width = factor.shape[1] // 2
    in_proj = jnp.dot(
        inputs_here.reshape(examples * length, shard_width),
        factor[:, :factor_width],
        preferred_element_type=jnp.float32,
    )
    out_proj = jnp.dot(
        grads_here.reshape(examples * length, shard_width),
        factor[:, factor_width:],
        preferred_element_type=jnp.float32,
    )
    return jnp.concatenate([in_proj, out_proj], axis=1)


def outer_features(token_rows, examples, length, factor_width):
    grouped = token_rows.reshape(examples, length, 2 * factor_width)
    outer = jnp.einsum(
        "esa,esb->eab",
        grouped[..., factor_width:],
        grouped[..., :factor_width],
        precision=lax.Precision.HIGHEST,
    ) / math.sqrt(length)
    return outer.reshape(examples, factor_width * factor_width).astype(jnp.bfloat16)


def local(train_inputs, train_grads, bench_inputs, bench_grads, answer_mask, factors, precond):
    factor = factors[0]
    factor_width = factor.shape[1] // 2
    length = train_inputs.shape[2]
    masked = bench_grads[0] * answer_mask.astype(jnp.bfloat16)[:, :, None]
    train_rows = project(train_inputs[0], train_grads[0], factor)
    bench_rows = project(bench_inputs[0], masked, factor)
    tensor_count = lax.axis_size("tensor")
    train_each = train_inputs.shape[1] // tensor_count
    bench_each = bench_inputs.shape[1] // tensor_count
    row_width = train_rows.shape[1]
    blocks = jnp.concatenate(
        [
            train_rows.reshape(tensor_count, train_each * length, row_width),
            bench_rows.reshape(tensor_count, bench_each * length, row_width),
        ],
        axis=1,
    ).reshape(-1, row_width)
    share_rows = blocks.shape[0] // tensor_count
    summed = lax.psum(blocks, "tensor")
    own_rows = lax.dynamic_slice_in_dim(
        summed, lax.axis_index("tensor") * share_rows, share_rows, 0
    )
    train_feats = outer_features(own_rows[: train_each * length], train_each, length, factor_width)
    bench_feats = outer_features(own_rows[train_each * length :], bench_each, length, factor_width)
    columns = precond[0]
    pre_cols = jnp.dot(
        lax.all_gather(bench_feats, ("dp", "tensor"), axis=0, tiled=True),
        columns,
        preferred_element_type=jnp.float32,
    ).astype(jnp.bfloat16)
    layer_total = lax.axis_size("layer") * train_inputs.shape[0]
    score_scale = 1.0 / math.sqrt(factor_width * factor_width * layer_total)
    whole_pre = lax.all_gather(pre_cols, ("dp", "tensor"), axis=1, tiled=True)
    partial_value = jnp.einsum(
        "ek,jk->ej", train_feats, whole_pre, preferred_element_type=jnp.float32
    )
    scores = lax.psum_scatter(partial_value, "layer", scatter_dimension=0, tiled=True)
    return scores * score_scale


def fused_kernel(
    dims,
    ti, tg, bi, bg, mask, fac, pre,
    out,
    bench_v, train_v, fac_v, mask_v, pre_v,
    bench_part, bench_send, bench_recv, train_part, train_recv,
    proj, feats, t_send, t_all, partial_v, score_recv,
    load_sem, swap_send, swap_recv, gather_send, gather_recv,
    t_send_sem, t_recv_sem, score_send, score_recv_sem,
):
    n_dp, scale = dims
    f32, bf16 = jnp.float32, jnp.bfloat16
    z, x, layer = lax.axis_index("dp"), lax.axis_index("tensor"), lax.axis_index("layer")
    other = 1 - x
    slots = 2 * n_dp
    length = mask.shape[1]
    shard = fac.shape[0]
    columns = pre_v.shape[1]
    width = 64
    tile = 8 * length
    along = (((1,), (1,)), ((), ()))

    def load(source, target, index):
        copy = pltpu.make_async_copy(source, target, load_sem.at[index])
        copy.start()
        return copy

    def rows_of(ref, piece):
        return ref.at[pl.ds(pl.multiple_of(piece * tile, tile), tile), :]

    mask_load = load(mask, mask_v, 0)
    fac_load = load(fac, fac_v, 1)
    bench_loads = [
        [load(rows_of(ref, b), bench_v.at[b, i], 2 + 2 * b + i) for i, ref in enumerate((bi, bg))]
        for b in range(2)
    ]
    train_loads = [
        [
            load(rows_of(ref, piece), train_v.at[b, i], 6 + 2 * b + i)
            for i, ref in enumerate((ti, tg))
        ]
        for b, piece in enumerate((2 * other, 2 * other + 1, 2 * x, 2 * x + 1))
    ]
    pre_load = load(pre, pre_v, 14)

    steps = [(dz, dx) for dz in range(n_dp) for dx in range(2)]

    def device(dz, dx, dl):
        where = {}
        if dz:
            where["dp"] = lax.rem(z + dz, n_dp)
        if dx:
            where["tensor"] = other
        if dl:
            where["layer"] = 1 - layer
        return where

    barrier = pltpu.get_barrier_semaphore()
    for dz, dx in steps:
        for dl in range(2):
            if dz or dx or dl:
                pl.semaphore_signal(
                    barrier, inc=1, device_id=device(dz, dx, dl), device_id_type=MESH
                )

    def remote(source, target, send, recv, where):
        return pltpu.make_async_remote_copy(
            source, target, send, recv, device_id=where, device_id_type=MESH
        )

    lane8 = lax.broadcasted_iota(jnp.int32, (8, tile), 1)
    row8 = lax.broadcasted_iota(jnp.int32, (8, tile), 0)
    same = lane8 // length == row8
    block = jnp.where(same, 1.0 / math.sqrt(length), 0.0)

    def project(ref):
        both = jnp.dot(
            ref[...].reshape(2 * tile, shard), fac_v[...], preferred_element_type=f32
        )
        lane = lax.broadcasted_iota(jnp.int32, (tile, 128), 1)
        return jnp.where(lane < width, both[:tile], both[tile:])

    def spread(rows):
        whole = jnp.broadcast_to(rows[:, None, :], (width, 8, tile)) * block[None]
        pairs = whole.reshape(width // 2, 2, 8, tile)
        even = pairs[:, 0].reshape(width * 4, tile)
        odd = pairs[:, 1].reshape(width * 4, tile)
        return jnp.concatenate([even, odd], axis=1)

    def paired(rows):
        zero = jnp.zeros_like(rows)
        return jnp.concatenate(
            [jnp.concatenate([rows, zero], axis=1), jnp.concatenate([zero, rows], axis=1)], axis=0
        )

    def outer(left, right):
        return lax.dot_general(left, right, along, preferred_element_type=f32).reshape(
            width // 2, 8, 128
        )

    def bench_outer(ref):
        tokens = ref[...]
        return outer(spread(tokens[width:].astype(f32)).astype(bf16), paired(tokens[:width]))

    def train_outer(whole):
        left, right = spread(whole[width:]), paired(whole[:width])
        left_high, right_high = left.astype(bf16), right.astype(bf16)
        left_low = (left - left_high.astype(f32)).astype(bf16)
        right_low = (right - right_high.astype(f32)).astype(bf16)
        return outer(
            jnp.concatenate([left_high, left_low, left_high], axis=1),
            jnp.concatenate([right_high, right_high, right_low], axis=1),
        )

    with jax.named_scope("keep"):
        mask_load.wait()
        keeps = []
        lay = jnp.where(
            lax.broadcasted_iota(jnp.int32, (length, tile), 1) % length
            == lax.broadcasted_iota(jnp.int32, (length, tile), 0),
            1.0, 0.0,
        ).astype(bf16)
        for b in range(2):
            flags = mask_v[pl.ds(8 * b, 8), :].astype(f32)
            tiled = jnp.dot(flags.astype(bf16), lay, preferred_element_type=f32)
            masked = jnp.where(same, tiled, 0.0).astype(bf16)
            keeps.append(jnp.dot(jnp.ones((width, 8), bf16), masked, preferred_element_type=f32))

    bench_swaps = [
        remote(bench_send.at[b], bench_recv.at[b], swap_send.at[b], swap_recv.at[b], device(0, 1, 0))
        for b in range(2)
    ]
    train_swaps = [
        remote(
            train_part.at[b], train_recv.at[b], swap_send.at[2 + b], swap_recv.at[2 + b],
            device(0, 1, 0),
        )
        for b in range(2)
    ]

    with jax.named_scope("fac_wait"):
        fac_load.wait()
    for b in range(2):
        with jax.named_scope("bench_load_wait"):
            for one in bench_loads[b]:
                one.wait()
        with jax.named_scope("bench_project"):
            value = project(bench_v.at[b])
            bench_part[b] = value
            bench_send[b] = value.astype(bf16)
        if b == 0:
            with jax.named_scope("barrier"):
                pl.semaphore_wait(barrier, 2 * slots - 1)
        bench_swaps[b].start()

    def train_project(b):
        with jax.named_scope("train_load_wait"):
            for one in train_loads[b]:
                one.wait()
        with jax.named_scope("train_project"):
            train_part[b] = project(train_v.at[b])

    for b in range(2):
        train_project(b)
        train_swaps[b].start()

    gathers = []
    for b in range(2):
        with jax.named_scope("bench_swap_wait"):
            bench_swaps[b].wait_recv()
        with jax.named_scope("bench_turn"):
            turned = (bench_part[b] + bench_recv[b].astype(f32)).T
            proj[z, b] = jnp.concatenate(
                [turned[:width], turned[width:] * keeps[b]], axis=0
            ).astype(bf16)
        for dz in [n_dp // 2] + [d for d in range(1, n_dp) if d != n_dp // 2]:
            one = remote(
                proj.at[z, b], proj.at[z, b], gather_send.at[b, dz], gather_recv.at[b, dz],
                device(dz, 0, 0),
            )
            one.start()
            gathers.append(one)

    for b in range(2):
        train_project(2 + b)

    def bench_feats(slot):
        with jax.named_scope("bench_feats"):
            both = jnp.concatenate(
                [bench_outer(proj.at[slot, 0]), bench_outer(proj.at[slot, 1])], axis=1
            ).astype(bf16)
            for p in range(width // 2):
                feats[slot, :, p * 128 : p * 128 + 128] = both[p]

    bench_feats(z)

    halves = []
    for b in range(2):
        with jax.named_scope("train_swap_wait"):
            train_swaps[b].wait_recv()
        with jax.named_scope("train_feats"):
            halves.append(train_outer((train_part[2 + b] + train_recv[b]).T))
    with jax.named_scope("train_store"):
        both = jnp.concatenate(halves, axis=1).astype(bf16)
        per_slot = columns // 128
        for p in range(width // 2):
            at = p % per_slot * 128
            t_send[p // per_slot, :, at : at + 128] = both[p]

    def t_copy(r, dz, dx):
        target = lax.rem(z + dz, n_dp) * 2 + lax.rem(x + dx, 2)
        return remote(
            t_send.at[target], t_all.at[r], t_send_sem.at[r], t_recv_sem.at[r], device(dz, dx, 0)
        )

    t_copies = [t_copy(r, dz, dx) for r, (dz, dx) in enumerate(steps) if r]
    for one in t_copies:
        one.start()
    t_all[0] = t_send[z * 2 + x]

    for dz in [d for d in range(1, n_dp) if d != n_dp // 2] + [n_dp // 2]:
        slot = lax.rem(z + n_dp - dz, n_dp)
        with jax.named_scope("gather_wait"):
            for b in range(2):
                remote(
                    proj.at[slot, b], proj.at[slot, b], gather_send.at[b, dz], gather_recv.at[b, dz],
                    device(dz, 0, 0),
                ).wait_recv()
        bench_feats(slot)

    with jax.named_scope("pre_wait"):
        pre_load.wait()
    with jax.named_scope("pre_dot"):
        bench_pre = jnp.dot(
            feats[...].reshape(n_dp * 16, feats.shape[2]), pre_v[...], preferred_element_type=f32
        )
        pre_high = bench_pre.astype(bf16)
        pre_low = (bench_pre - pre_high.astype(f32)).astype(bf16)
        pre_both = jnp.concatenate([pre_high, pre_low], axis=0)

    with jax.named_scope("t_wait"):
        for one in t_copies:
            one.wait_recv()
    with jax.named_scope("score_dot"):
        held = t_all[...].reshape(slots * 16, columns)
        wide = lax.dot_general(held, pre_both, along, preferred_element_type=f32)
        partial_v[...] = (wide + pltpu.roll(wide, n_dp * 16, 1)).reshape(slots, 2, 8, 128)

    score_copies = []
    for r, (dz, dx) in enumerate(steps):
        for dl in range(2):
            if dz or dx or dl:
                half = layer if dl == 0 else 1 - layer
                one = remote(
                    partial_v.at[r, half], score_recv.at[r, dl],
                    score_send.at[r, dl], score_recv_sem.at[r, dl],
                    device((n_dp - dz) % n_dp, dx, dl),
                )
                score_copies.append((r, dl, one))
    with jax.named_scope("score_start"):
        for r, dl, one in reversed(score_copies):
            one.start()
    result = partial_v[0, layer]
    with jax.named_scope("score_wait"):
        for r, dl, one in score_copies:
            one.wait_recv()
            result = result + score_recv[r, dl]
    out[...] = result[:, : out.shape[1]] * scale

    with jax.named_scope("send_wait"):
        for one in bench_swaps + train_swaps + gathers + t_copies + [c for _, _, c in score_copies]:
            one.wait_send()


def fused(train_inputs, train_grads, bench_inputs, bench_grads, answer_mask, factors, precond):
    f32, bf16 = jnp.float32, jnp.bfloat16
    _, train, length, shard = train_inputs.shape
    bench = bench_inputs.shape[1]
    n_dp = lax.axis_size("dp")
    slots = 2 * n_dp
    features, columns = precond.shape[1:]
    scale = 1.0 / math.sqrt(features * lax.axis_size("layer"))
    tile = 8 * length
    dma = pltpu.SemaphoreType.DMA
    anywhere = pl.BlockSpec(memory_space=pl.ANY)
    return pl.pallas_call(
        functools.partial(fused_kernel, (n_dp, scale)),
        out_shape=jax.ShapeDtypeStruct((8, n_dp * bench), f32),
        in_specs=[anywhere] * 7,
        out_specs=pl.BlockSpec(memory_space=pltpu.VMEM),
        scratch_shapes=[
            pltpu.VMEM((2, 2, tile, shard), bf16),
            pltpu.VMEM((4, 2, tile, shard), bf16),
            pltpu.VMEM((shard, 128), bf16),
            pltpu.VMEM((bench, length), jnp.int32),
            pltpu.VMEM((features, columns), bf16),
            pltpu.VMEM((2, tile, 128), f32),
            pltpu.VMEM((2, tile, 128), bf16),
            pltpu.VMEM((2, tile, 128), bf16),
            pltpu.VMEM((4, tile, 128), f32),
            pltpu.VMEM((2, tile, 128), f32),
            pltpu.VMEM((n_dp, 2, 128, tile), bf16),
            pltpu.VMEM((n_dp, bench, features), bf16),
            pltpu.VMEM((slots, 16, columns), bf16),
            pltpu.VMEM((slots, 16, columns), bf16),
            pltpu.VMEM((slots, 2, 8, 128), f32),
            pltpu.VMEM((slots, 2, 8, 128), f32),
            dma((15,)),
            dma((4,)),
            dma((4,)),
            dma((2, n_dp)),
            dma((2, n_dp)),
            dma((slots,)),
            dma((slots,)),
            dma((slots, 2)),
            dma((slots, 2)),
        ],
        compiler_params=pltpu.CompilerParams(
            collective_id=0, has_side_effects=True, vmem_limit_bytes=56 * 1024 * 1024
        ),
    )(
        train_inputs.reshape(train * length, shard),
        train_grads.reshape(train * length, shard),
        bench_inputs.reshape(bench * length, shard),
        bench_grads.reshape(bench * length, shard),
        answer_mask,
        factors[0],
        precond[0],
    )


def fits(shapes, sizes):
    train, bench, length, shard, half_width, features, columns, layers = shapes
    n_dp, n_tensor, n_layer = sizes
    return (
        n_tensor == 2 and n_layer == 2 and layers == 1 and half_width == 64 and length == 16
        and bench == 16 and train == 32 and n_dp == 4
        and shard % 256 == 0 and columns % 128 == 0 and features == 4096
        and features == 2 * n_dp * columns
    )


def local_any(*args):
    train_inputs, _, bench_inputs, _, _, factors, precond = args
    shapes = (
        train_inputs.shape[1], bench_inputs.shape[1], train_inputs.shape[2], train_inputs.shape[3],
        factors.shape[2] // 2, precond.shape[1], precond.shape[2], train_inputs.shape[0],
    )
    sizes = tuple(lax.axis_size(name) for name in ("dp", "tensor", "layer"))
    return fused(*args) if fits(shapes, sizes) else local(*args)


def solution(mesh):
    placed = (
        P("layer", ("groups", "dp"), None, "tensor"),
        P("layer", ("groups", "dp"), None, "tensor"),
        P("layer", ("groups", "dp"), None, "tensor"),
        P("layer", ("groups", "dp"), None, "tensor"),
        P(("groups", "dp"), None),
        P("layer", "tensor", None),
        P("layer", None, ("dp", "tensor")),
    )
    return jax.shard_map(
        local_any,
        mesh=mesh,
        in_specs=placed,
        out_specs=P(("groups", "dp", "tensor", "layer"), None),
        check_vma=False,
    )
```

```python
import functools
import math

import jax
import jax.numpy as jnp
from jax import lax
from jax.experimental import pallas as pl
from jax.experimental.pallas import tpu as pltpu
from jax.sharding import PartitionSpec as P

MESH = pl.DeviceIdType.MESH


def project(inputs_here, grads_here, factor):
    examples, length, shard_width = inputs_here.shape
    factor_width = factor.shape[1] // 2
    in_proj = jnp.dot(
        inputs_here.reshape(examples * length, shard_width),
        factor[:, :factor_width],
        preferred_element_type=jnp.float32,
    )
    out_proj = jnp.dot(
        grads_here.reshape(examples * length, shard_width),
        factor[:, factor_width:],
        preferred_element_type=jnp.float32,
    )
    return jnp.concatenate([in_proj, out_proj], axis=1)


def outer_features(token_rows, examples, length, factor_width):
    grouped = token_rows.reshape(examples, length, 2 * factor_width)
    outer = jnp.einsum(
        "esa,esb->eab",
        grouped[..., factor_width:],
        grouped[..., :factor_width],
        precision=lax.Precision.HIGHEST,
    ) / math.sqrt(length)
    return outer.reshape(examples, factor_width * factor_width).astype(jnp.bfloat16)


def local(train_inputs, train_grads, bench_inputs, bench_grads, answer_mask, factors, precond):
    factor = factors[0]
    factor_width = factor.shape[1] // 2
    length = train_inputs.shape[2]
    masked = bench_grads[0] * answer_mask.astype(jnp.bfloat16)[:, :, None]
    train_rows = project(train_inputs[0], train_grads[0], factor)
    bench_rows = project(bench_inputs[0], masked, factor)
    tensor_count = lax.axis_size("tensor")
    train_each = train_inputs.shape[1] // tensor_count
    bench_each = bench_inputs.shape[1] // tensor_count
    row_width = train_rows.shape[1]
    blocks = jnp.concatenate(
        [
            train_rows.reshape(tensor_count, train_each * length, row_width),
            bench_rows.reshape(tensor_count, bench_each * length, row_width),
        ],
        axis=1,
    ).reshape(-1, row_width)
    share_rows = blocks.shape[0] // tensor_count
    summed = lax.psum(blocks, "tensor")
    own_rows = lax.dynamic_slice_in_dim(
        summed, lax.axis_index("tensor") * share_rows, share_rows, 0
    )
    train_feats = outer_features(own_rows[: train_each * length], train_each, length, factor_width)
    bench_feats = outer_features(own_rows[train_each * length :], bench_each, length, factor_width)
    columns = precond[0]
    pre_cols = jnp.dot(
        lax.all_gather(bench_feats, ("dp", "tensor"), axis=0, tiled=True),
        columns,
        preferred_element_type=jnp.float32,
    ).astype(jnp.bfloat16)
    layer_total = lax.axis_size("layer") * train_inputs.shape[0]
    score_scale = 1.0 / math.sqrt(factor_width * factor_width * layer_total)
    whole_pre = lax.all_gather(pre_cols, ("dp", "tensor"), axis=1, tiled=True)
    partial_value = jnp.einsum(
        "ek,jk->ej", train_feats, whole_pre, preferred_element_type=jnp.float32
    )
    scores = lax.psum_scatter(partial_value, "layer", scatter_dimension=0, tiled=True)
    return scores * score_scale


def fused_kernel(
    dims,
    ti, tg, bi, bg, mask, fac, pre,
    out,
    bench_v, train_v, fac_v, mask_v, pre_v,
    bench_part, bench_send, bench_recv, train_part, train_recv,
    proj, feats, t_send, t_all, partial_v, score_recv,
    load_sem, swap_recv, gather_recv, late_recv, send_sem,
):
    n_dp, scale = dims
    f32, bf16 = jnp.float32, jnp.bfloat16
    z, x, layer = lax.axis_index("dp"), lax.axis_index("tensor"), lax.axis_index("layer")
    other = 1 - x
    slots = 2 * n_dp
    length = mask.shape[1]
    shard = fac.shape[0]
    columns = pre_v.shape[1]
    width = 64
    tile = 8 * length
    along = (((1,), (1,)), ((), ()))

    def load(source, target, index):
        copy = pltpu.make_async_copy(source, target, load_sem.at[index])
        copy.start()
        return copy

    def rows_of(ref, piece):
        return ref.at[pl.ds(pl.multiple_of(piece * tile, tile), tile), :]

    mask_load = load(mask, mask_v, 0)
    fac_load = load(fac, fac_v, 1)
    for b in range(2):
        for i, ref in enumerate((bi, bg)):
            load(rows_of(ref, b), bench_v.at[b, i], 2 + b)
    for b, piece in enumerate((2 * other, 2 * other + 1, 2 * x, 2 * x + 1)):
        for i, ref in enumerate((ti, tg)):
            load(rows_of(ref, piece), train_v.at[b, i], 4 + b)
    pre_load = load(pre, pre_v, 8)

    def landed(ref, sem):
        pltpu.make_async_copy(ref, ref, sem).wait()

    steps = [(dz, dx) for dz in range(n_dp) for dx in range(2)]

    def device(dz, dx, dl):
        where = {}
        if dz:
            where["dp"] = lax.rem(z + dz, n_dp)
        if dx:
            where["tensor"] = other
        if dl:
            where["layer"] = 1 - layer
        return where

    barrier = pltpu.get_barrier_semaphore()
    for dz, dx in steps:
        for dl in range(2):
            if dz or dx or dl:
                pl.semaphore_signal(
                    barrier, inc=1, device_id=device(dz, dx, dl), device_id_type=MESH
                )

    def remote(source, target, send, recv, where):
        return pltpu.make_async_remote_copy(
            source, target, send, recv, device_id=where, device_id_type=MESH
        )

    lane8 = lax.broadcasted_iota(jnp.int32, (8, tile), 1)
    row8 = lax.broadcasted_iota(jnp.int32, (8, tile), 0)
    same = lane8 // length == row8
    block = jnp.where(same, 1.0 / math.sqrt(length), 0.0)

    def project(ref):
        both = jnp.dot(
            ref[...].reshape(2 * tile, shard), fac_v[...], preferred_element_type=f32
        )
        lane = lax.broadcasted_iota(jnp.int32, (tile, 128), 1)
        return jnp.where(lane < width, both[:tile], both[tile:])

    def spread(rows):
        whole = jnp.broadcast_to(rows[:, None, :], (width, 8, tile)) * block[None]
        pairs = whole.reshape(width // 2, 2, 8, tile)
        even = pairs[:, 0].reshape(width * 4, tile)
        odd = pairs[:, 1].reshape(width * 4, tile)
        return jnp.concatenate([even, odd], axis=1)

    def paired(rows):
        zero = jnp.zeros_like(rows)
        return jnp.concatenate(
            [jnp.concatenate([rows, zero], axis=1), jnp.concatenate([zero, rows], axis=1)], axis=0
        )

    def outer(left, right):
        return lax.dot_general(left, right, along, preferred_element_type=f32).reshape(
            width // 2, 8, 128
        )

    def bench_outer(ref):
        tokens = ref[...]
        return outer(spread(tokens[width:].astype(f32)).astype(bf16), paired(tokens[:width]))

    def train_outer(whole):
        left, right = spread(whole[width:]), paired(whole[:width])
        left_high, right_high = left.astype(bf16), right.astype(bf16)
        left_low = (left - left_high.astype(f32)).astype(bf16)
        right_low = (right - right_high.astype(f32)).astype(bf16)
        return outer(
            jnp.concatenate([left_high, left_low, left_high], axis=1),
            jnp.concatenate([right_high, right_high, right_low], axis=1),
        )

    with jax.named_scope("keep"):
        mask_load.wait()
        keeps = []
        lay = jnp.where(
            lax.broadcasted_iota(jnp.int32, (length, tile), 1) % length
            == lax.broadcasted_iota(jnp.int32, (length, tile), 0),
            1.0, 0.0,
        ).astype(bf16)
        for b in range(2):
            flags = mask_v[pl.ds(8 * b, 8), :].astype(f32)
            tiled = jnp.dot(flags.astype(bf16), lay, preferred_element_type=f32)
            masked = jnp.where(same, tiled, 0.0).astype(bf16)
            keeps.append(jnp.dot(jnp.ones((width, 8), bf16), masked, preferred_element_type=f32))

    bench_swaps = [
        remote(bench_send.at[b], bench_recv.at[b], send_sem.at[0], swap_recv.at[b], device(0, 1, 0))
        for b in range(2)
    ]
    train_swaps = [
        remote(
            train_part.at[b], train_recv.at[b], send_sem.at[1], swap_recv.at[2 + b],
            device(0, 1, 0),
        )
        for b in range(2)
    ]

    with jax.named_scope("fac_wait"):
        fac_load.wait()
    for b in range(2):
        with jax.named_scope("bench_load_wait"):
            landed(bench_v.at[b], load_sem.at[2 + b])
        with jax.named_scope("bench_project"):
            value = project(bench_v.at[b])
            bench_part[b] = value
            bench_send[b] = value.astype(bf16)
        if b == 0:
            with jax.named_scope("barrier"):
                pl.semaphore_wait(barrier, 2 * slots - 1)
        bench_swaps[b].start()

    def train_project(b):
        with jax.named_scope("train_load_wait"):
            landed(train_v.at[b], load_sem.at[4 + b])
        with jax.named_scope("train_project"):
            train_part[b] = project(train_v.at[b])

    for b in range(2):
        train_project(b)
        train_swaps[b].start()

    for b in range(2):
        with jax.named_scope("bench_swap_wait"):
            bench_swaps[b].wait_recv()
        with jax.named_scope("bench_turn"):
            turned = (bench_part[b] + bench_recv[b].astype(f32)).T
            proj[z, b] = jnp.concatenate(
                [turned[:width], turned[width:] * keeps[b]], axis=0
            ).astype(bf16)
        for dz in [n_dp // 2] + [d for d in range(1, n_dp) if d != n_dp // 2]:
            one = remote(
                proj.at[z, b], proj.at[z, b], send_sem.at[2], gather_recv.at[dz], device(dz, 0, 0)
            )
            one.start()

    for b in range(2):
        train_project(2 + b)

    def bench_feats(slot):
        with jax.named_scope("bench_feats"):
            both = jnp.concatenate(
                [bench_outer(proj.at[slot, 0]), bench_outer(proj.at[slot, 1])], axis=1
            ).astype(bf16)
            for p in range(width // 2):
                feats[slot, :, p * 128 : p * 128 + 128] = both[p]

    bench_feats(z)

    halves = []
    for b in range(2):
        with jax.named_scope("train_swap_wait"):
            train_swaps[b].wait_recv()
        with jax.named_scope("train_feats"):
            halves.append(train_outer((train_part[2 + b] + train_recv[b]).T))
    with jax.named_scope("train_store"):
        both = jnp.concatenate(halves, axis=1).astype(bf16)
        per_slot = columns // 128
        for p in range(width // 2):
            at = p % per_slot * 128
            t_send[p // per_slot, :, at : at + 128] = both[p]

    def t_copy(r, dz, dx):
        target = lax.rem(z + dz, n_dp) * 2 + lax.rem(x + dx, 2)
        return remote(
            t_send.at[target], t_all.at[r], send_sem.at[3], late_recv.at[0], device(dz, dx, 0)
        )

    t_copies = [t_copy(r, dz, dx) for r, (dz, dx) in enumerate(steps) if r]
    for one in t_copies:
        one.start()
    t_all[0] = t_send[z * 2 + x]

    for dz in [d for d in range(1, n_dp) if d != n_dp // 2] + [n_dp // 2]:
        slot = lax.rem(z + n_dp - dz, n_dp)
        with jax.named_scope("gather_wait"):
            landed(proj.at[slot], gather_recv.at[dz])
        bench_feats(slot)

    with jax.named_scope("pre_wait"):
        pre_load.wait()
    with jax.named_scope("pre_dot"):
        bench_pre = jnp.dot(
            feats[...].reshape(n_dp * 16, feats.shape[2]), pre_v[...], preferred_element_type=f32
        )
        pre_high = bench_pre.astype(bf16)
        pre_low = (bench_pre - pre_high.astype(f32)).astype(bf16)
        pre_both = jnp.concatenate([pre_high, pre_low], axis=0)

    with jax.named_scope("t_wait"):
        landed(t_all.at[pl.ds(1, slots - 1)], late_recv.at[0])
    with jax.named_scope("score_dot"):
        held = t_all[...].reshape(slots * 16, columns)
        wide = lax.dot_general(held, pre_both, along, preferred_element_type=f32)
        partial_v[...] = (wide + pltpu.roll(wide, n_dp * 16, 1)).reshape(2 * slots, 8, 128)

    score_copies = []
    for r, (dz, dx) in enumerate(steps):
        for dl in range(2):
            if dz or dx or dl:
                half = layer if dl == 0 else 1 - layer
                one = remote(
                    partial_v.at[2 * r + half], score_recv.at[2 * r + dl],
                    send_sem.at[4], late_recv.at[1], device((n_dp - dz) % n_dp, dx, dl),
                )
                score_copies.append(one)
    with jax.named_scope("score_start"):
        for one in reversed(score_copies):
            one.start()
    with jax.named_scope("score_wait"):
        landed(score_recv.at[pl.ds(1, 2 * slots - 1)], late_recv.at[1])
    result = partial_v[layer]
    for index in range(1, 2 * slots):
        result = result + score_recv[index]
    out[...] = result[:, : out.shape[1]] * scale

    with jax.named_scope("send_wait"):
        landed(bench_send, send_sem.at[0])
        landed(train_part.at[pl.ds(0, 2)], send_sem.at[1])
        landed(proj.at[pl.ds(0, n_dp - 1)], send_sem.at[2])
        landed(t_send.at[pl.ds(0, slots - 1)], send_sem.at[3])
        landed(partial_v.at[pl.ds(0, 2 * slots - 1)], send_sem.at[4])


def fused(train_inputs, train_grads, bench_inputs, bench_grads, answer_mask, factors, precond):
    f32, bf16 = jnp.float32, jnp.bfloat16
    _, train, length, shard = train_inputs.shape
    bench = bench_inputs.shape[1]
    n_dp = lax.axis_size("dp")
    slots = 2 * n_dp
    features, columns = precond.shape[1:]
    scale = 1.0 / math.sqrt(features * lax.axis_size("layer"))
    tile = 8 * length
    dma = pltpu.SemaphoreType.DMA
    anywhere = pl.BlockSpec(memory_space=pl.ANY)
    return pl.pallas_call(
        functools.partial(fused_kernel, (n_dp, scale)),
        out_shape=pltpu.VMEM((8, n_dp * bench), f32),
        in_specs=[anywhere] * 7,
        out_specs=pl.BlockSpec(memory_space=pltpu.VMEM),
        scratch_shapes=[
            pltpu.VMEM((2, 2, tile, shard), bf16),
            pltpu.VMEM((4, 2, tile, shard), bf16),
            pltpu.VMEM((shard, 128), bf16),
            pltpu.VMEM((bench, length), jnp.int32),
            pltpu.VMEM((features, columns), bf16),
            pltpu.VMEM((2, tile, 128), f32),
            pltpu.VMEM((2, tile, 128), bf16),
            pltpu.VMEM((2, tile, 128), bf16),
            pltpu.VMEM((4, tile, 128), f32),
            pltpu.VMEM((2, tile, 128), f32),
            pltpu.VMEM((n_dp, 2, 128, tile), bf16),
            pltpu.VMEM((n_dp, bench, features), bf16),
            pltpu.VMEM((slots, 16, columns), bf16),
            pltpu.VMEM((slots, 16, columns), bf16),
            pltpu.VMEM((2 * slots, 8, 128), f32),
            pltpu.VMEM((2 * slots, 8, 128), f32),
            dma((9,)),
            dma((4,)),
            dma((n_dp,)),
            dma((2,)),
            dma((5,)),
        ],
        compiler_params=pltpu.CompilerParams(
            collective_id=0, has_side_effects=True, vmem_limit_bytes=56 * 1024 * 1024
        ),
    )(
        train_inputs.reshape(train * length, shard),
        train_grads.reshape(train * length, shard),
        bench_inputs.reshape(bench * length, shard),
        bench_grads.reshape(bench * length, shard),
        answer_mask,
        factors[0],
        precond[0],
    )


def fits(shapes, sizes):
    train, bench, length, shard, half_width, features, columns, layers = shapes
    n_dp, n_tensor, n_layer = sizes
    return (
        n_tensor == 2 and n_layer == 2 and layers == 1 and half_width == 64 and length == 16
        and bench == 16 and train == 32 and n_dp == 4
        and shard % 256 == 0 and columns % 128 == 0 and features == 4096
        and features == 2 * n_dp * columns
    )


def local_any(*args):
    train_inputs, _, bench_inputs, _, _, factors, precond = args
    shapes = (
        train_inputs.shape[1], bench_inputs.shape[1], train_inputs.shape[2], train_inputs.shape[3],
        factors.shape[2] // 2, precond.shape[1], precond.shape[2], train_inputs.shape[0],
    )
    sizes = tuple(lax.axis_size(name) for name in ("dp", "tensor", "layer"))
    return fused(*args) if fits(shapes, sizes) else local(*args)


def solution(mesh):
    placed = (
        P("layer", ("groups", "dp"), None, "tensor"),
        P("layer", ("groups", "dp"), None, "tensor"),
        P("layer", ("groups", "dp"), None, "tensor"),
        P("layer", ("groups", "dp"), None, "tensor"),
        P(("groups", "dp"), None),
        P("layer", "tensor", None),
        P("layer", None, ("dp", "tensor")),
    )
    return jax.shard_map(
        local_any,
        mesh=mesh,
        in_specs=placed,
        out_specs=P(("groups", "dp", "tensor", "layer"), None),
        check_vma=False,
    )
```

```python
import functools
import math

import jax
import jax.numpy as jnp
from jax import lax
from jax.experimental import pallas as pl
from jax.experimental.pallas import tpu as pltpu
from jax.sharding import PartitionSpec as P

MESH = pl.DeviceIdType.MESH


def project(inputs_here, grads_here, factor):
    examples, length, shard_width = inputs_here.shape
    factor_width = factor.shape[1] // 2
    in_proj = jnp.dot(
        inputs_here.reshape(examples * length, shard_width),
        factor[:, :factor_width],
        preferred_element_type=jnp.float32,
    )
    out_proj = jnp.dot(
        grads_here.reshape(examples * length, shard_width),
        factor[:, factor_width:],
        preferred_element_type=jnp.float32,
    )
    return jnp.concatenate([in_proj, out_proj], axis=1)


def outer_features(token_rows, examples, length, factor_width):
    grouped = token_rows.reshape(examples, length, 2 * factor_width)
    outer = jnp.einsum(
        "esa,esb->eab",
        grouped[..., factor_width:],
        grouped[..., :factor_width],
        precision=lax.Precision.HIGHEST,
    ) / math.sqrt(length)
    return outer.reshape(examples, factor_width * factor_width).astype(jnp.bfloat16)


def local(train_inputs, train_grads, bench_inputs, bench_grads, answer_mask, factors, precond):
    factor = factors[0]
    factor_width = factor.shape[1] // 2
    length = train_inputs.shape[2]
    masked = bench_grads[0] * answer_mask.astype(jnp.bfloat16)[:, :, None]
    train_rows = project(train_inputs[0], train_grads[0], factor)
    bench_rows = project(bench_inputs[0], masked, factor)
    tensor_count = lax.axis_size("tensor")
    train_each = train_inputs.shape[1] // tensor_count
    bench_each = bench_inputs.shape[1] // tensor_count
    row_width = train_rows.shape[1]
    blocks = jnp.concatenate(
        [
            train_rows.reshape(tensor_count, train_each * length, row_width),
            bench_rows.reshape(tensor_count, bench_each * length, row_width),
        ],
        axis=1,
    ).reshape(-1, row_width)
    share_rows = blocks.shape[0] // tensor_count
    summed = lax.psum(blocks, "tensor")
    own_rows = lax.dynamic_slice_in_dim(
        summed, lax.axis_index("tensor") * share_rows, share_rows, 0
    )
    train_feats = outer_features(own_rows[: train_each * length], train_each, length, factor_width)
    bench_feats = outer_features(own_rows[train_each * length :], bench_each, length, factor_width)
    columns = precond[0]
    pre_cols = jnp.dot(
        lax.all_gather(bench_feats, ("dp", "tensor"), axis=0, tiled=True),
        columns,
        preferred_element_type=jnp.float32,
    ).astype(jnp.bfloat16)
    layer_total = lax.axis_size("layer") * train_inputs.shape[0]
    score_scale = 1.0 / math.sqrt(factor_width * factor_width * layer_total)
    whole_pre = lax.all_gather(pre_cols, ("dp", "tensor"), axis=1, tiled=True)
    partial_value = jnp.einsum(
        "ek,jk->ej", train_feats, whole_pre, preferred_element_type=jnp.float32
    )
    scores = lax.psum_scatter(partial_value, "layer", scatter_dimension=0, tiled=True)
    return scores * score_scale


def fused_kernel(
    dims,
    ti, tg, bi, bg, mask, fac, pre,
    out,
    bench_v, train_v, fac_v, mask_v, pre_v,
    bench_part, bench_send, bench_recv, train_part, train_recv,
    proj, feats, t_send, t_all, partial_v, score_recv,
    load_sem, swap_recv, gather_recv, t_recv, score_sem, send_sem,
):
    n_dp, scale = dims
    f32, bf16 = jnp.float32, jnp.bfloat16
    z, x, layer = lax.axis_index("dp"), lax.axis_index("tensor"), lax.axis_index("layer")
    other = 1 - x
    me = z * 2 + x
    slots = 2 * n_dp
    length = mask.shape[1]
    shard = fac.shape[0]
    columns = pre_v.shape[1]
    width = 64
    tile = 8 * length
    piece = tile // 2
    along = (((1,), (1,)), ((), ()))

    def load(source, target, index):
        copy = pltpu.make_async_copy(source, target, load_sem.at[index])
        copy.start()
        return copy

    def rows_of(ref, index, rows):
        return ref.at[pl.ds(pl.multiple_of(index * rows, rows), rows), :]

    mask_load = load(mask, mask_v, 0)
    fac_load = load(fac, fac_v, 1)
    for q in range(4):
        for i, ref in enumerate((bi, bg)):
            load(rows_of(ref, q, piece), bench_v.at[q, i], 2 + q)
    for b, index in enumerate((2 * other, 2 * other + 1, 2 * x, 2 * x + 1)):
        for i, ref in enumerate((ti, tg)):
            load(rows_of(ref, index, tile), train_v.at[b, i], 6 + b)
    pre_load = load(pre, pre_v, 10)

    def landed(ref, sem):
        pltpu.make_async_copy(ref, ref, sem).wait()

    near = jnp.where(2 * z < n_dp, z, n_dp - 1 - z)

    def line(i):
        place = jnp.where(near <= i, i + 1, i)
        return jnp.where(2 * z < n_dp, place, n_dp - 1 - place)

    others = [line(i) for i in range(n_dp - 1)]

    stage = jnp.where(z > 1, 0, jnp.where(z + x > 0, 1, 2))

    barrier = pltpu.get_barrier_semaphore()
    for where in [{"dp": one} for one in others] + [{"tensor": other}, {"layer": 1 - layer}]:
        pl.semaphore_signal(barrier, inc=1, device_id=where, device_id_type=MESH)

    def remote(source, target, send, recv, where):
        return pltpu.make_async_remote_copy(
            source, target, send, recv, device_id=where, device_id_type=MESH
        )

    lane8 = lax.broadcasted_iota(jnp.int32, (8, tile), 1)
    row8 = lax.broadcasted_iota(jnp.int32, (8, tile), 0)
    root = 1.0 / math.sqrt(length)
    train_block = jnp.where(lane8 // length == row8, root, 0.0)
    bench_block = jnp.where((lane8 // length + 4) % 8 == row8, root, 0.0)

    def project(ref):
        rows = ref.shape[1]
        both = jnp.dot(
            ref[...].reshape(2 * rows, shard), fac_v[...], preferred_element_type=f32
        )
        lane = lax.broadcasted_iota(jnp.int32, (rows, 128), 1)
        return jnp.where(lane < width, both[:rows], both[rows:])

    def spread(rows, block):
        whole = jnp.broadcast_to(rows[:, None, :], (width, 8, tile)) * block[None]
        pairs = whole.reshape(width // 2, 2, 8, tile)
        even = pairs[:, 0].reshape(width * 4, tile)
        odd = pairs[:, 1].reshape(width * 4, tile)
        return jnp.concatenate([even, odd], axis=1)

    def paired(rows):
        zero = jnp.zeros_like(rows)
        return jnp.concatenate(
            [jnp.concatenate([rows, zero], axis=1), jnp.concatenate([zero, rows], axis=1)], axis=0
        )

    def outer(left, right):
        return lax.dot_general(left, right, along, preferred_element_type=f32).reshape(
            width // 2, 8, 128
        )

    def bench_outer(first, second):
        first, second = first[...].astype(f32), second[...].astype(f32)
        lane = lax.broadcasted_iota(jnp.int32, first.shape, 1)
        ins = jnp.where(lane < width, second, pltpu.roll(first, width, 1))
        outs = jnp.where(lane < width, pltpu.roll(second, width, 1), first)
        return outer(spread(outs, bench_block).astype(bf16), paired(ins).astype(bf16))

    def train_outer(whole):
        left, right = spread(whole[width:], train_block), paired(whole[:width])
        left_high, right_high = left.astype(bf16), right.astype(bf16)
        left_low = (left - left_high.astype(f32)).astype(bf16)
        right_low = (right - right_high.astype(f32)).astype(bf16)
        return outer(
            jnp.concatenate([left_high, left_low, left_high], axis=1),
            jnp.concatenate([right_high, right_high, right_low], axis=1),
        )

    with jax.named_scope("keep"):
        mask_load.wait()
        keeps = []
        lay = jnp.where(
            lax.broadcasted_iota(jnp.int32, (length, tile), 1) % length
            == lax.broadcasted_iota(jnp.int32, (length, tile), 0),
            1.0, 0.0,
        ).astype(bf16)
        for q in range(4):
            flags = mask_v[pl.ds(q // 2 * 8, 8), :].astype(f32).astype(bf16)
            tiled = jnp.dot(flags, lay, preferred_element_type=f32)
            wanted = (lane8 >= width) & ((lane8 - width) // length + 4 * (q % 2) == row8)
            masked = jnp.where(wanted, tiled, jnp.where((lane8 < width) & (row8 == 0), 1.0, 0.0))
            keeps.append(
                jnp.dot(jnp.ones((width, 8), bf16), masked.astype(bf16), preferred_element_type=f32)
            )

    bench_swaps = [
        remote(
            bench_send.at[q], bench_recv.at[q], send_sem.at[0], swap_recv.at[q], {"tensor": other}
        )
        for q in range(4)
    ]
    train_swaps = [
        remote(
            train_part.at[b], train_recv.at[b], send_sem.at[1], swap_recv.at[4 + b],
            {"tensor": other},
        )
        for b in range(2)
    ]

    with jax.named_scope("fac_wait"):
        fac_load.wait()
    for q in range(4):
        with jax.named_scope("bench_load_wait"):
            landed(bench_v.at[q], load_sem.at[2 + q])
        with jax.named_scope("bench_project"):
            value = project(bench_v.at[q])
            bench_part[q] = value
            bench_send[q] = value.astype(bf16)

        @pl.when(stage == 0)
        def _(q=q):
            if q == 0:
                pl.semaphore_wait(barrier, n_dp + 1)
            bench_swaps[q].start()

    @pl.when(stage == 1)
    def _():
        pl.semaphore_wait(barrier, n_dp + 1)
        for one in bench_swaps:
            one.start()

    def train_project(b):
        with jax.named_scope("train_load_wait"):
            landed(train_v.at[b], load_sem.at[6 + b])
        with jax.named_scope("train_project"):
            train_part[b] = project(train_v.at[b])

    for b in range(2):
        train_project(b)

        @pl.when((stage < 2) & (layer == 0))
        def _(b=b):
            train_swaps[b].start()

    @pl.when(stage == 2)
    def _():
        pl.semaphore_wait(barrier, n_dp + 1)
        for one in bench_swaps:
            one.start()

    @pl.when((stage == 2) & (layer == 0))
    def _():
        for one in train_swaps:
            one.start()

    @pl.when(stage == 2)
    def _():
        for b in range(2):
            train_project(2 + b)

    for q in range(4):
        with jax.named_scope("bench_swap_wait"):
            bench_swaps[q].wait_recv()
        with jax.named_scope("bench_turn"):
            turned = (bench_part[q] + bench_recv[q].astype(f32)).T
            proj[z, q] = (
                jnp.concatenate([turned[:width], turned[width:]], axis=1) * keeps[q]
            ).astype(bf16)
        for one in reversed(others):
            remote(
                proj.at[z, q], proj.at[z, q], send_sem.at[2], gather_recv.at[z], {"dp": one}
            ).start()

    @pl.when(layer == 1)
    def _():
        for one in train_swaps:
            one.start()

    @pl.when(stage < 2)
    def _():
        for b in range(2):
            train_project(2 + b)

    def bench_feats(slot):
        with jax.named_scope("bench_feats"):
            both = jnp.concatenate(
                [bench_outer(proj.at[slot, 2 * h], proj.at[slot, 2 * h + 1]) for h in range(2)],
                axis=1,
            ).astype(bf16)
            for p in range(width // 2):
                feats[slot, :, p * 128 : p * 128 + 128] = both[p]

    halves = []
    for b in range(2):
        with jax.named_scope("train_swap_wait"):
            train_swaps[b].wait_recv()
        with jax.named_scope("train_feats"):
            halves.append(train_outer((train_part[2 + b] + train_recv[b]).T))
    with jax.named_scope("train_store"):
        both = jnp.concatenate(halves, axis=1).astype(bf16)
        per_slot = columns // 128
        for p in range(width // 2):
            at = p % per_slot * 128
            t_send[p // per_slot, :, at : at + 128] = both[p]

    def t_copy(target, where):
        remote(t_send.at[target], t_all.at[me], send_sem.at[3], t_recv.at[z], where).start()

    def t_start():
        for one in reversed(others):
            for column in range(2):
                t_copy(one * 2 + column, {"dp": one, "tensor": column})
        t_copy(z * 2 + other, {"tensor": other})

    pl.when(layer == 0)(t_start)
    pltpu.make_async_copy(t_send.at[me], t_all.at[me], t_recv.at[z]).start()
    bench_feats(z)

    for index in [0] + list(range(n_dp - 2, 0, -1)):
        slot = others[index]
        with jax.named_scope("gather_wait"):
            landed(proj.at[slot], gather_recv.at[slot])
        if index == 1:
            pl.when(layer == 1)(t_start)
        bench_feats(slot)

    with jax.named_scope("pre_wait"):
        pre_load.wait()
    with jax.named_scope("pre_dot"):
        bench_pre = jnp.dot(
            feats[...].reshape(n_dp * 16, feats.shape[2]), pre_v[...], preferred_element_type=f32
        )
        pre_high = bench_pre.astype(bf16)
        pre_low = (bench_pre - pre_high.astype(f32)).astype(bf16)
        pre_both = jnp.concatenate([pre_high, pre_low], axis=0)

    own = me * 2 + layer
    for at in range(n_dp):
        with jax.named_scope("t_wait"):
            landed(t_all.at[pl.ds(2 * at, 2)], t_recv.at[at])
        with jax.named_scope("score_dot"):
            held = t_all[2 * at : 2 * at + 2].reshape(32, columns)
            wide = lax.dot_general(held, pre_both, along, preferred_element_type=f32)
            partial_v[4 * at : 4 * at + 4] = (wide + pltpu.roll(wide, n_dp * 16, 1)).reshape(4, 8, 128)
        for column, core in ((other, 1 - layer), (other, layer), (x, 1 - layer)):
            remote(
                partial_v.at[4 * at + 2 * column + core], score_recv.at[own],
                send_sem.at[4], score_sem.at[0],
                {"dp": at, "tensor": column, "layer": core},
            ).start()
        mine = partial_v.at[4 * at + 2 * x + layer]

        @pl.when(z == at)
        def _():
            pltpu.make_async_copy(mine, score_recv.at[own], score_sem.at[0]).start()

        @pl.when(z != at)
        def _():
            remote(mine, score_recv.at[own], send_sem.at[4], score_sem.at[0], {"dp": at}).start()

    with jax.named_scope("score_wait"):
        landed(score_recv, score_sem.at[0])
    result = score_recv[0]
    for index in range(1, 2 * slots):
        result = result + score_recv[index]
    out[...] = result[:, : out.shape[1]] * scale

    with jax.named_scope("send_wait"):
        landed(bench_send, send_sem.at[0])
        landed(train_part.at[pl.ds(0, 2)], send_sem.at[1])
        landed(proj.at[pl.ds(0, n_dp - 1)], send_sem.at[2])
        landed(t_send.at[pl.ds(0, slots - 1)], send_sem.at[3])
        landed(partial_v.at[pl.ds(0, 2 * slots - 1)], send_sem.at[4])


def fused(train_inputs, train_grads, bench_inputs, bench_grads, answer_mask, factors, precond):
    f32, bf16 = jnp.float32, jnp.bfloat16
    _, train, length, shard = train_inputs.shape
    bench = bench_inputs.shape[1]
    n_dp = lax.axis_size("dp")
    slots = 2 * n_dp
    features, columns = precond.shape[1:]
    scale = 1.0 / math.sqrt(features * lax.axis_size("layer"))
    tile = 8 * length
    dma = pltpu.SemaphoreType.DMA
    anywhere = pl.BlockSpec(memory_space=pl.ANY)
    return pl.pallas_call(
        functools.partial(fused_kernel, (n_dp, scale)),
        out_shape=pltpu.VMEM((8, n_dp * bench), f32),
        in_specs=[anywhere] * 7,
        out_specs=pl.BlockSpec(memory_space=pltpu.VMEM),
        scratch_shapes=[
            pltpu.VMEM((4, 2, tile // 2, shard), bf16),
            pltpu.VMEM((4, 2, tile, shard), bf16),
            pltpu.VMEM((shard, 128), bf16),
            pltpu.VMEM((bench, length), jnp.int32),
            pltpu.VMEM((features, columns), bf16),
            pltpu.VMEM((4, tile // 2, 128), f32),
            pltpu.VMEM((4, tile // 2, 128), bf16),
            pltpu.VMEM((4, tile // 2, 128), bf16),
            pltpu.VMEM((4, tile, 128), f32),
            pltpu.VMEM((2, tile, 128), f32),
            pltpu.VMEM((n_dp, 4, 64, 128), bf16),
            pltpu.VMEM((n_dp, bench, features), bf16),
            pltpu.VMEM((slots, 16, columns), bf16),
            pltpu.VMEM((slots, 16, columns), bf16),
            pltpu.VMEM((2 * slots, 8, 128), f32),
            pltpu.VMEM((2 * slots, 8, 128), f32),
            dma((11,)),
            dma((6,)),
            dma((n_dp,)),
            dma((n_dp,)),
            dma((1,)),
            dma((5,)),
        ],
        compiler_params=pltpu.CompilerParams(
            collective_id=0, has_side_effects=True, vmem_limit_bytes=56 * 1024 * 1024
        ),
    )(
        train_inputs.reshape(train * length, shard),
        train_grads.reshape(train * length, shard),
        bench_inputs.reshape(bench * length, shard),
        bench_grads.reshape(bench * length, shard),
        answer_mask,
        factors[0],
        precond[0],
    )


def fits(shapes, sizes):
    train, bench, length, shard, half_width, features, columns, layers = shapes
    n_dp, n_tensor, n_layer = sizes
    return (
        n_tensor == 2 and n_layer == 2 and layers == 1 and half_width == 64 and length == 16
        and bench == 16 and train == 32 and n_dp == 4
        and shard % 256 == 0 and columns % 128 == 0 and features == 4096
        and features == 2 * n_dp * columns
    )


def local_any(*args):
    train_inputs, _, bench_inputs, _, _, factors, precond = args
    shapes = (
        train_inputs.shape[1], bench_inputs.shape[1], train_inputs.shape[2], train_inputs.shape[3],
        factors.shape[2] // 2, precond.shape[1], precond.shape[2], train_inputs.shape[0],
    )
    sizes = tuple(lax.axis_size(name) for name in ("dp", "tensor", "layer"))
    return fused(*args) if fits(shapes, sizes) else local(*args)


def solution(mesh):
    placed = (
        P("layer", ("groups", "dp"), None, "tensor"),
        P("layer", ("groups", "dp"), None, "tensor"),
        P("layer", ("groups", "dp"), None, "tensor"),
        P("layer", ("groups", "dp"), None, "tensor"),
        P(("groups", "dp"), None),
        P("layer", "tensor", None),
        P("layer", None, ("dp", "tensor")),
    )
    return jax.shard_map(
        local_any,
        mesh=mesh,
        in_specs=placed,
        out_specs=P(("groups", "dp", "tensor", "layer"), None),
        check_vma=False,
    )
```

```python
import functools
import math

import jax
import jax.numpy as jnp
from jax import lax
from jax.experimental import pallas as pl
from jax.experimental.pallas import tpu as pltpu
from jax.sharding import PartitionSpec as P

MESH = pl.DeviceIdType.MESH


def project(inputs_here, grads_here, factor):
    examples, length, shard_width = inputs_here.shape
    factor_width = factor.shape[1] // 2
    in_proj = jnp.dot(
        inputs_here.reshape(examples * length, shard_width),
        factor[:, :factor_width],
        preferred_element_type=jnp.float32,
    )
    out_proj = jnp.dot(
        grads_here.reshape(examples * length, shard_width),
        factor[:, factor_width:],
        preferred_element_type=jnp.float32,
    )
    return jnp.concatenate([in_proj, out_proj], axis=1)


def outer_features(token_rows, examples, length, factor_width):
    grouped = token_rows.reshape(examples, length, 2 * factor_width)
    outer = jnp.einsum(
        "esa,esb->eab",
        grouped[..., factor_width:],
        grouped[..., :factor_width],
        precision=lax.Precision.HIGHEST,
    ) / math.sqrt(length)
    return outer.reshape(examples, factor_width * factor_width).astype(jnp.bfloat16)


def local(train_inputs, train_grads, bench_inputs, bench_grads, answer_mask, factors, precond):
    factor = factors[0]
    factor_width = factor.shape[1] // 2
    length = train_inputs.shape[2]
    masked = bench_grads[0] * answer_mask.astype(jnp.bfloat16)[:, :, None]
    train_rows = project(train_inputs[0], train_grads[0], factor)
    bench_rows = project(bench_inputs[0], masked, factor)
    tensor_count = lax.axis_size("tensor")
    train_each = train_inputs.shape[1] // tensor_count
    bench_each = bench_inputs.shape[1] // tensor_count
    row_width = train_rows.shape[1]
    blocks = jnp.concatenate(
        [
            train_rows.reshape(tensor_count, train_each * length, row_width),
            bench_rows.reshape(tensor_count, bench_each * length, row_width),
        ],
        axis=1,
    ).reshape(-1, row_width)
    share_rows = blocks.shape[0] // tensor_count
    summed = lax.psum(blocks, "tensor")
    own_rows = lax.dynamic_slice_in_dim(
        summed, lax.axis_index("tensor") * share_rows, share_rows, 0
    )
    train_feats = outer_features(own_rows[: train_each * length], train_each, length, factor_width)
    bench_feats = outer_features(own_rows[train_each * length :], bench_each, length, factor_width)
    columns = precond[0]
    pre_cols = jnp.dot(
        lax.all_gather(bench_feats, ("dp", "tensor"), axis=0, tiled=True),
        columns,
        preferred_element_type=jnp.float32,
    ).astype(jnp.bfloat16)
    layer_total = lax.axis_size("layer") * train_inputs.shape[0]
    score_scale = 1.0 / math.sqrt(factor_width * factor_width * layer_total)
    whole_pre = lax.all_gather(pre_cols, ("dp", "tensor"), axis=1, tiled=True)
    partial_value = jnp.einsum(
        "ek,jk->ej", train_feats, whole_pre, preferred_element_type=jnp.float32
    )
    scores = lax.psum_scatter(partial_value, "layer", scatter_dimension=0, tiled=True)
    return scores * score_scale


def fused_kernel(
    dims,
    ti, tg, bi, bg, mask, fac, pre,
    out,
    bench_v, train_v, fac_v, mask_v, pre_v,
    bench_part, bench_send, bench_recv, train_part, train_recv,
    proj, feats, t_send, t_all, partial_v, score_recv,
    load_sem, swap_recv, gather_recv, forward_recv, t_recv, score_sem, send_sem,
):
    n_dp, scale = dims
    f32, bf16 = jnp.float32, jnp.bfloat16
    z, x, layer = lax.axis_index("dp"), lax.axis_index("tensor"), lax.axis_index("layer")
    other = 1 - x
    me = z * 2 + x
    slots = 2 * n_dp
    length = mask.shape[1]
    shard = fac.shape[0]
    columns = pre_v.shape[1]
    width = 64
    tile = 8 * length
    piece = tile // 2
    along = (((1,), (1,)), ((), ()))

    def load(source, target, index):
        copy = pltpu.make_async_copy(source, target, load_sem.at[index])
        copy.start()
        return copy

    def rows_of(ref, index, rows):
        return ref.at[pl.ds(pl.multiple_of(index * rows, rows), rows), :]

    mask_load = load(mask, mask_v, 0)
    fac_load = load(fac, fac_v, 1)
    for q in range(4):
        for i, ref in enumerate((bi, bg)):
            load(rows_of(ref, q, piece), bench_v.at[q, i], 2 + q)
    for b, index in enumerate((2 * other, 2 * other + 1, 2 * x, 2 * x + 1)):
        for i, ref in enumerate((ti, tg)):
            load(rows_of(ref, index, tile), train_v.at[b, i], 6 + b)
    pre_load = load(pre, pre_v, 10)

    def landed(ref, sem):
        pltpu.make_async_copy(ref, ref, sem).wait()

    near = jnp.where(2 * z < n_dp, z, n_dp - 1 - z)

    def line(i):
        place = jnp.where(near <= i, i + 1, i)
        return jnp.where(2 * z < n_dp, place, n_dp - 1 - place)

    others = [line(i) for i in range(n_dp - 1)]

    stage = jnp.where(z > 1, 0, jnp.where(z + x > 0, 1, 2))

    barrier = pltpu.get_barrier_semaphore()
    for where in [{"dp": one} for one in others] + [{"tensor": other}, {"layer": 1 - layer}]:
        pl.semaphore_signal(barrier, inc=1, device_id=where, device_id_type=MESH)

    def remote(source, target, send, recv, where):
        return pltpu.make_async_remote_copy(
            source, target, send, recv, device_id=where, device_id_type=MESH
        )

    lane8 = lax.broadcasted_iota(jnp.int32, (8, tile), 1)
    row8 = lax.broadcasted_iota(jnp.int32, (8, tile), 0)
    root = 1.0 / math.sqrt(length)
    train_block = jnp.where(lane8 // length == row8, root, 0.0)
    bench_block = jnp.where((lane8 // length + 4) % 8 == row8, root, 0.0)

    def project(ref):
        rows = ref.shape[1]
        both = jnp.dot(
            ref[...].reshape(2 * rows, shard), fac_v[...], preferred_element_type=f32
        )
        lane = lax.broadcasted_iota(jnp.int32, (rows, 128), 1)
        return jnp.where(lane < width, both[:rows], both[rows:])

    def spread(rows, block):
        whole = jnp.broadcast_to(rows[:, None, :], (width, 8, tile)) * block[None]
        pairs = whole.reshape(width // 2, 2, 8, tile)
        even = pairs[:, 0].reshape(width * 4, tile)
        odd = pairs[:, 1].reshape(width * 4, tile)
        return jnp.concatenate([even, odd], axis=1)

    def paired(rows):
        zero = jnp.zeros_like(rows)
        return jnp.concatenate(
            [jnp.concatenate([rows, zero], axis=1), jnp.concatenate([zero, rows], axis=1)], axis=0
        )

    def outer(left, right):
        return lax.dot_general(left, right, along, preferred_element_type=f32).reshape(
            width // 2, 8, 128
        )

    def bench_outer(first, second):
        first, second = first[...].astype(f32), second[...].astype(f32)
        lane = lax.broadcasted_iota(jnp.int32, first.shape, 1)
        ins = jnp.where(lane < width, second, pltpu.roll(first, width, 1))
        outs = jnp.where(lane < width, pltpu.roll(second, width, 1), first)
        return outer(spread(outs, bench_block).astype(bf16), paired(ins).astype(bf16))

    def train_outer(whole):
        left, right = spread(whole[width:], train_block), paired(whole[:width])
        left_high, right_high = left.astype(bf16), right.astype(bf16)
        left_low = (left - left_high.astype(f32)).astype(bf16)
        right_low = (right - right_high.astype(f32)).astype(bf16)
        return outer(
            jnp.concatenate([left_high, left_low, left_high], axis=1),
            jnp.concatenate([right_high, right_high, right_low], axis=1),
        )

    with jax.named_scope("keep"):
        mask_load.wait()
        keeps = []
        lay = jnp.where(
            lax.broadcasted_iota(jnp.int32, (length, tile), 1) % length
            == lax.broadcasted_iota(jnp.int32, (length, tile), 0),
            1.0, 0.0,
        ).astype(bf16)
        for q in range(4):
            flags = mask_v[pl.ds(q // 2 * 8, 8), :].astype(f32).astype(bf16)
            tiled = jnp.dot(flags, lay, preferred_element_type=f32)
            wanted = (lane8 >= width) & ((lane8 - width) // length + 4 * (q % 2) == row8)
            masked = jnp.where(wanted, tiled, jnp.where((lane8 < width) & (row8 == 0), 1.0, 0.0))
            keeps.append(
                jnp.dot(jnp.ones((width, 8), bf16), masked.astype(bf16), preferred_element_type=f32)
            )

    bench_swaps = [
        remote(
            bench_send.at[q], bench_recv.at[q], send_sem.at[0], swap_recv.at[q], {"tensor": other}
        )
        for q in range(4)
    ]
    train_swaps = [
        remote(
            train_part.at[b], train_recv.at[b], send_sem.at[1], swap_recv.at[4 + b],
            {"tensor": other},
        )
        for b in range(2)
    ]

    with jax.named_scope("fac_wait"):
        fac_load.wait()
    for q in range(4):
        with jax.named_scope("bench_load_wait"):
            landed(bench_v.at[q], load_sem.at[2 + q])
        with jax.named_scope("bench_project"):
            value = project(bench_v.at[q])
            bench_part[q] = value
            bench_send[q] = value.astype(bf16)

        @pl.when(stage == 0)
        def _(q=q):
            if q == 0:
                pl.semaphore_wait(barrier, n_dp + 1)
            bench_swaps[q].start()

    @pl.when(stage == 1)
    def _():
        pl.semaphore_wait(barrier, n_dp + 1)
        for one in bench_swaps:
            one.start()

    def train_project(b):
        with jax.named_scope("train_load_wait"):
            landed(train_v.at[b], load_sem.at[6 + b])
        with jax.named_scope("train_project"):
            train_part[b] = project(train_v.at[b])

    for b in range(2):
        train_project(b)

        @pl.when((stage < 2) & (layer == 0))
        def _(b=b):
            train_swaps[b].start()

    @pl.when(stage == 2)
    def _():
        pl.semaphore_wait(barrier, n_dp + 1)
        for one in bench_swaps:
            one.start()

    @pl.when((stage == 2) & (layer == 0))
    def _():
        for one in train_swaps:
            one.start()

    @pl.when(stage == 2)
    def _():
        for b in range(2):
            train_project(2 + b)

    for q in range(4):
        with jax.named_scope("bench_swap_wait"):
            bench_swaps[q].wait_recv()
        with jax.named_scope("bench_turn"):
            turned = (bench_part[q] + bench_recv[q].astype(f32)).T
            proj[z, q] = (
                jnp.concatenate([turned[:width], turned[width:]], axis=1) * keeps[q]
            ).astype(bf16)

        @pl.when((layer == 0) | (x == q // 2))
        def _(q=q):
            for one in reversed(others):
                remote(
                    proj.at[z, q], proj.at[z, q], send_sem.at[2], gather_recv.at[z], {"dp": one}
                ).start()

    @pl.when(layer == 1)
    def _():
        for one in train_swaps:
            one.start()

    @pl.when(stage < 2)
    def _():
        for b in range(2):
            train_project(2 + b)

    def bench_feats(slot):
        with jax.named_scope("bench_feats"):
            both = jnp.concatenate(
                [bench_outer(proj.at[slot, 2 * h], proj.at[slot, 2 * h + 1]) for h in range(2)],
                axis=1,
            ).astype(bf16)
            for p in range(width // 2):
                feats[slot, :, p * 128 : p * 128 + 128] = both[p]

    order = [others[0]] + others[:0:-1]

    @pl.when(layer == 1)
    def _():
        for slot in order:
            half = proj.at[slot, pl.ds(2 * x, 2)]
            landed(half, gather_recv.at[slot])
            remote(half, half, send_sem.at[2], forward_recv.at[slot], {"tensor": other}).start()

    halves = []
    for b in range(2):
        with jax.named_scope("train_swap_wait"):
            train_swaps[b].wait_recv()
        with jax.named_scope("train_feats"):
            halves.append(train_outer((train_part[2 + b] + train_recv[b]).T))
    with jax.named_scope("train_store"):
        both = jnp.concatenate(halves, axis=1).astype(bf16)
        per_slot = columns // 128
        for p in range(width // 2):
            at = p % per_slot * 128
            t_send[p // per_slot, :, at : at + 128] = both[p]

    def t_copy(target, where):
        remote(t_send.at[target], t_all.at[me], send_sem.at[3], t_recv.at[z], where).start()

    for one in reversed(others):
        for column in range(2):
            t_copy(one * 2 + column, {"dp": one, "tensor": column})
    t_copy(z * 2 + other, {"tensor": other})
    pltpu.make_async_copy(t_send.at[me], t_all.at[me], t_recv.at[z]).start()
    bench_feats(z)

    for slot in order:
        with jax.named_scope("gather_wait"):

            @pl.when(layer == 0)
            def _(slot=slot):
                landed(proj.at[slot], gather_recv.at[slot])

            @pl.when(layer == 1)
            def _(slot=slot):
                landed(proj.at[slot, pl.ds(0, 2)], forward_recv.at[slot])

        bench_feats(slot)

    with jax.named_scope("pre_wait"):
        pre_load.wait()
    with jax.named_scope("pre_dot"):
        bench_pre = jnp.dot(
            feats[...].reshape(n_dp * 16, feats.shape[2]), pre_v[...], preferred_element_type=f32
        )
        pre_high = bench_pre.astype(bf16)
        pre_low = (bench_pre - pre_high.astype(f32)).astype(bf16)
        pre_both = jnp.concatenate([pre_high, pre_low], axis=0)

    own = me * 2 + layer
    for at in range(n_dp):
        with jax.named_scope("t_wait"):
            landed(t_all.at[pl.ds(2 * at, 2)], t_recv.at[at])
        with jax.named_scope("score_dot"):
            held = t_all[2 * at : 2 * at + 2].reshape(32, columns)
            wide = lax.dot_general(held, pre_both, along, preferred_element_type=f32)
            partial_v[4 * at : 4 * at + 4] = (wide + pltpu.roll(wide, n_dp * 16, 1)).reshape(4, 8, 128)
        for column, core in ((other, 1 - layer), (other, layer), (x, 1 - layer)):
            remote(
                partial_v.at[4 * at + 2 * column + core], score_recv.at[own],
                send_sem.at[4], score_sem.at[0],
                {"dp": at, "tensor": column, "layer": core},
            ).start()
        mine = partial_v.at[4 * at + 2 * x + layer]

        @pl.when(z == at)
        def _():
            pltpu.make_async_copy(mine, score_recv.at[own], score_sem.at[0]).start()

        @pl.when(z != at)
        def _():
            remote(mine, score_recv.at[own], send_sem.at[4], score_sem.at[0], {"dp": at}).start()

    with jax.named_scope("score_wait"):
        landed(score_recv, score_sem.at[0])
    result = score_recv[0]
    for index in range(1, 2 * slots):
        result = result + score_recv[index]
    out[...] = result[:, : out.shape[1]] * scale

    with jax.named_scope("send_wait"):
        landed(bench_send, send_sem.at[0])
        landed(train_part.at[pl.ds(0, 2)], send_sem.at[1])
        landed(proj.at[pl.ds(0, n_dp - 1)], send_sem.at[2])
        landed(t_send.at[pl.ds(0, slots - 1)], send_sem.at[3])
        landed(partial_v.at[pl.ds(0, 2 * slots - 1)], send_sem.at[4])


def fused(train_inputs, train_grads, bench_inputs, bench_grads, answer_mask, factors, precond):
    f32, bf16 = jnp.float32, jnp.bfloat16
    _, train, length, shard = train_inputs.shape
    bench = bench_inputs.shape[1]
    n_dp = lax.axis_size("dp")
    slots = 2 * n_dp
    features, columns = precond.shape[1:]
    scale = 1.0 / math.sqrt(features * lax.axis_size("layer"))
    tile = 8 * length
    dma = pltpu.SemaphoreType.DMA
    anywhere = pl.BlockSpec(memory_space=pl.ANY)
    return pl.pallas_call(
        functools.partial(fused_kernel, (n_dp, scale)),
        out_shape=pltpu.VMEM((8, n_dp * bench), f32),
        in_specs=[anywhere] * 7,
        out_specs=pl.BlockSpec(memory_space=pltpu.VMEM),
        scratch_shapes=[
            pltpu.VMEM((4, 2, tile // 2, shard), bf16),
            pltpu.VMEM((4, 2, tile, shard), bf16),
            pltpu.VMEM((shard, 128), bf16),
            pltpu.VMEM((bench, length), jnp.int32),
            pltpu.VMEM((features, columns), bf16),
            pltpu.VMEM((4, tile // 2, 128), f32),
            pltpu.VMEM((4, tile // 2, 128), bf16),
            pltpu.VMEM((4, tile // 2, 128), bf16),
            pltpu.VMEM((4, tile, 128), f32),
            pltpu.VMEM((2, tile, 128), f32),
            pltpu.VMEM((n_dp, 4, 64, 128), bf16),
            pltpu.VMEM((n_dp, bench, features), bf16),
            pltpu.VMEM((slots, 16, columns), bf16),
            pltpu.VMEM((slots, 16, columns), bf16),
            pltpu.VMEM((2 * slots, 8, 128), f32),
            pltpu.VMEM((2 * slots, 8, 128), f32),
            dma((11,)),
            dma((6,)),
            dma((n_dp,)),
            dma((n_dp,)),
            dma((n_dp,)),
            dma((1,)),
            dma((5,)),
        ],
        compiler_params=pltpu.CompilerParams(
            collective_id=0, has_side_effects=True, vmem_limit_bytes=56 * 1024 * 1024
        ),
    )(
        train_inputs.reshape(train * length, shard),
        train_grads.reshape(train * length, shard),
        bench_inputs.reshape(bench * length, shard),
        bench_grads.reshape(bench * length, shard),
        answer_mask,
        factors[0],
        precond[0],
    )


def fits(shapes, sizes):
    train, bench, length, shard, half_width, features, columns, layers = shapes
    n_dp, n_tensor, n_layer = sizes
    return (
        n_tensor == 2 and n_layer == 2 and layers == 1 and half_width == 64 and length == 16
        and bench == 16 and train == 32 and n_dp == 4
        and shard % 256 == 0 and columns % 128 == 0 and features == 4096
        and features == 2 * n_dp * columns
    )


def local_any(*args):
    train_inputs, _, bench_inputs, _, _, factors, precond = args
    shapes = (
        train_inputs.shape[1], bench_inputs.shape[1], train_inputs.shape[2], train_inputs.shape[3],
        factors.shape[2] // 2, precond.shape[1], precond.shape[2], train_inputs.shape[0],
    )
    sizes = tuple(lax.axis_size(name) for name in ("dp", "tensor", "layer"))
    return fused(*args) if fits(shapes, sizes) else local(*args)


def solution(mesh):
    placed = (
        P("layer", ("groups", "dp"), None, "tensor"),
        P("layer", ("groups", "dp"), None, "tensor"),
        P("layer", ("groups", "dp"), None, "tensor"),
        P("layer", ("groups", "dp"), None, "tensor"),
        P(("groups", "dp"), None),
        P("layer", "tensor", None),
        P("layer", None, ("dp", "tensor")),
    )
    return jax.shard_map(
        local_any,
        mesh=mesh,
        in_specs=placed,
        out_specs=P(("groups", "dp", "tensor", "layer"), None),
        check_vma=False,
    )
```

```python
import functools
import math

import jax
import jax.numpy as jnp
from jax import lax
from jax.experimental import pallas as pl
from jax.experimental.pallas import tpu as pltpu
from jax.sharding import PartitionSpec as P

MESH = pl.DeviceIdType.MESH


def project(inputs_here, grads_here, factor):
    examples, length, shard_width = inputs_here.shape
    factor_width = factor.shape[1] // 2
    in_proj = jnp.dot(
        inputs_here.reshape(examples * length, shard_width),
        factor[:, :factor_width],
        preferred_element_type=jnp.float32,
    )
    out_proj = jnp.dot(
        grads_here.reshape(examples * length, shard_width),
        factor[:, factor_width:],
        preferred_element_type=jnp.float32,
    )
    return jnp.concatenate([in_proj, out_proj], axis=1)


def outer_features(token_rows, examples, length, factor_width):
    grouped = token_rows.reshape(examples, length, 2 * factor_width)
    outer = jnp.einsum(
        "esa,esb->eab",
        grouped[..., factor_width:],
        grouped[..., :factor_width],
        precision=lax.Precision.HIGHEST,
    ) / math.sqrt(length)
    return outer.reshape(examples, factor_width * factor_width).astype(jnp.bfloat16)


def local(train_inputs, train_grads, bench_inputs, bench_grads, answer_mask, factors, precond):
    factor = factors[0]
    factor_width = factor.shape[1] // 2
    length = train_inputs.shape[2]
    masked = bench_grads[0] * answer_mask.astype(jnp.bfloat16)[:, :, None]
    train_rows = project(train_inputs[0], train_grads[0], factor)
    bench_rows = project(bench_inputs[0], masked, factor)
    tensor_count = lax.axis_size("tensor")
    train_each = train_inputs.shape[1] // tensor_count
    bench_each = bench_inputs.shape[1] // tensor_count
    row_width = train_rows.shape[1]
    blocks = jnp.concatenate(
        [
            train_rows.reshape(tensor_count, train_each * length, row_width),
            bench_rows.reshape(tensor_count, bench_each * length, row_width),
        ],
        axis=1,
    ).reshape(-1, row_width)
    share_rows = blocks.shape[0] // tensor_count
    summed = lax.psum(blocks, "tensor")
    own_rows = lax.dynamic_slice_in_dim(
        summed, lax.axis_index("tensor") * share_rows, share_rows, 0
    )
    train_feats = outer_features(own_rows[: train_each * length], train_each, length, factor_width)
    bench_feats = outer_features(own_rows[train_each * length :], bench_each, length, factor_width)
    columns = precond[0]
    pre_cols = jnp.dot(
        lax.all_gather(bench_feats, ("dp", "tensor"), axis=0, tiled=True),
        columns,
        preferred_element_type=jnp.float32,
    ).astype(jnp.bfloat16)
    layer_total = lax.axis_size("layer") * train_inputs.shape[0]
    score_scale = 1.0 / math.sqrt(factor_width * factor_width * layer_total)
    whole_pre = lax.all_gather(pre_cols, ("dp", "tensor"), axis=1, tiled=True)
    partial_value = jnp.einsum(
        "ek,jk->ej", train_feats, whole_pre, preferred_element_type=jnp.float32
    )
    scores = lax.psum_scatter(partial_value, "layer", scatter_dimension=0, tiled=True)
    return scores * score_scale


def fused_kernel(
    dims,
    ti, tg, bi, bg, mask, fac, pre,
    out,
    bench_v, train_v, fac_v, mask_v, pre_v,
    bench_part, bench_send, bench_recv, train_part, train_recv,
    proj, feats, t_send, t_all, partial_v, score_recv,
    load_sem, swap_recv, gather_recv, forward_recv, t_recv, score_sem, send_sem,
):
    n_dp, scale = dims
    f32, bf16 = jnp.float32, jnp.bfloat16
    z, x, layer = lax.axis_index("dp"), lax.axis_index("tensor"), lax.axis_index("layer")
    other = 1 - x
    me = z * 2 + x
    slots = 2 * n_dp
    length = mask.shape[1]
    shard = fac.shape[0]
    columns = pre_v.shape[1]
    width = 64
    tile = 8 * length
    piece = tile // 2
    along = (((1,), (1,)), ((), ()))

    def load(source, target, index):
        copy = pltpu.make_async_copy(source, target, load_sem.at[index])
        copy.start()
        return copy

    def rows_of(ref, index, rows):
        return ref.at[pl.ds(pl.multiple_of(index * rows, rows), rows), :]

    mask_load = load(mask, mask_v, 0)
    fac_load = load(fac, fac_v, 1)
    for q in range(4):
        for i, ref in enumerate((bi, bg)):
            load(rows_of(ref, q, piece), bench_v.at[q, i], 2 + q)
    for b, index in enumerate((2 * other, 2 * other + 1, 2 * x, 2 * x + 1)):
        for i, ref in enumerate((ti, tg)):
            load(rows_of(ref, index, tile), train_v.at[b, i], 6 + b)
    pre_load = load(pre, pre_v, 10)

    def landed(ref, sem):
        pltpu.make_async_copy(ref, ref, sem).wait()

    near = jnp.where(2 * z < n_dp, z, n_dp - 1 - z)

    def line(i):
        place = jnp.where(near <= i, i + 1, i)
        return jnp.where(2 * z < n_dp, place, n_dp - 1 - place)

    others = [line(i) for i in range(n_dp - 1)]

    stage = jnp.where(z > 1, 0, jnp.where(z + x > 0, 1, 2))

    barrier = pltpu.get_barrier_semaphore()
    for where in [{"dp": one} for one in others] + [{"tensor": other}, {"layer": 1 - layer}]:
        pl.semaphore_signal(barrier, inc=1, device_id=where, device_id_type=MESH)

    def remote(source, target, send, recv, where):
        return pltpu.make_async_remote_copy(
            source, target, send, recv, device_id=where, device_id_type=MESH
        )

    lane8 = lax.broadcasted_iota(jnp.int32, (8, tile), 1)
    row8 = lax.broadcasted_iota(jnp.int32, (8, tile), 0)
    root = 1.0 / math.sqrt(length)
    train_block = jnp.where(lane8 // length == row8, root, 0.0)
    bench_block = jnp.where((lane8 // length + 4) % 8 == row8, root, 0.0)

    def project(ref):
        rows = ref.shape[1]
        both = jnp.dot(
            ref[...].reshape(2 * rows, shard), fac_v[...], preferred_element_type=f32
        )
        lane = lax.broadcasted_iota(jnp.int32, (rows, 128), 1)
        return jnp.where(lane < width, both[:rows], both[rows:])

    def spread(rows, block):
        whole = jnp.broadcast_to(rows[:, None, :], (width, 8, tile)) * block[None]
        pairs = whole.reshape(width // 2, 2, 8, tile)
        even = pairs[:, 0].reshape(width * 4, tile)
        odd = pairs[:, 1].reshape(width * 4, tile)
        return jnp.concatenate([even, odd], axis=1)

    def paired(rows):
        zero = jnp.zeros_like(rows)
        return jnp.concatenate(
            [jnp.concatenate([rows, zero], axis=1), jnp.concatenate([zero, rows], axis=1)], axis=0
        )

    def outer(left, right):
        return lax.dot_general(left, right, along, preferred_element_type=f32).reshape(
            width // 2, 8, 128
        )

    def bench_outer(first, second):
        first, second = first[...].astype(f32), second[...].astype(f32)
        lane = lax.broadcasted_iota(jnp.int32, first.shape, 1)
        ins = jnp.where(lane < width, second, pltpu.roll(first, width, 1))
        outs = jnp.where(lane < width, pltpu.roll(second, width, 1), first)
        return outer(spread(outs, bench_block).astype(bf16), paired(ins).astype(bf16))

    def train_outer(whole):
        left, right = spread(whole[width:], train_block), paired(whole[:width])
        left_high, right_high = left.astype(bf16), right.astype(bf16)
        left_low = (left - left_high.astype(f32)).astype(bf16)
        right_low = (right - right_high.astype(f32)).astype(bf16)
        return outer(
            jnp.concatenate([left_high, left_low, left_high], axis=1),
            jnp.concatenate([right_high, right_high, right_low], axis=1),
        )

    with jax.named_scope("keep"):
        mask_load.wait()
        keeps = []
        lay = jnp.where(
            lax.broadcasted_iota(jnp.int32, (length, tile), 1) % length
            == lax.broadcasted_iota(jnp.int32, (length, tile), 0),
            1.0, 0.0,
        ).astype(bf16)
        for q in range(4):
            flags = mask_v[pl.ds(q // 2 * 8, 8), :].astype(f32).astype(bf16)
            tiled = jnp.dot(flags, lay, preferred_element_type=f32)
            wanted = (lane8 >= width) & ((lane8 - width) // length + 4 * (q % 2) == row8)
            masked = jnp.where(wanted, tiled, jnp.where((lane8 < width) & (row8 == 0), 1.0, 0.0))
            keeps.append(
                jnp.dot(jnp.ones((width, 8), bf16), masked.astype(bf16), preferred_element_type=f32)
            )

    bench_swaps = [
        remote(
            bench_send.at[q], bench_recv.at[q], send_sem.at[0], swap_recv.at[q], {"tensor": other}
        )
        for q in range(4)
    ]
    train_swaps = [
        remote(
            train_part.at[b], train_recv.at[b], send_sem.at[1], swap_recv.at[4 + b],
            {"tensor": other},
        )
        for b in range(2)
    ]

    with jax.named_scope("fac_wait"):
        fac_load.wait()
    for q in range(4):
        with jax.named_scope("bench_load_wait"):
            landed(bench_v.at[q], load_sem.at[2 + q])
        with jax.named_scope("bench_project"):
            value = project(bench_v.at[q])
            bench_part[q] = value
            bench_send[q] = value.astype(bf16)

        @pl.when(stage == 0)
        def _(q=q):
            if q == 0:
                pl.semaphore_wait(barrier, n_dp + 1)
            bench_swaps[q].start()

    @pl.when(stage == 1)
    def _():
        pl.semaphore_wait(barrier, n_dp + 1)
        for one in bench_swaps:
            one.start()

    def train_project(b):
        with jax.named_scope("train_load_wait"):
            landed(train_v.at[b], load_sem.at[6 + b])
        with jax.named_scope("train_project"):
            train_part[b] = project(train_v.at[b])

    for b in range(2):
        train_project(b)

        @pl.when((stage < 2) & (layer == 0))
        def _(b=b):
            train_swaps[b].start()

    @pl.when(stage == 2)
    def _():
        pl.semaphore_wait(barrier, n_dp + 1)
        for one in bench_swaps:
            one.start()

    @pl.when((stage == 2) & (layer == 0))
    def _():
        for one in train_swaps:
            one.start()

    @pl.when(stage == 2)
    def _():
        for b in range(2):
            train_project(2 + b)

    for q in range(4):
        with jax.named_scope("bench_swap_wait"):
            bench_swaps[q].wait_recv()
        with jax.named_scope("bench_turn"):
            turned = (bench_part[q] + bench_recv[q].astype(f32)).T
            proj[z, q] = (
                jnp.concatenate([turned[:width], turned[width:]], axis=1) * keeps[q]
            ).astype(bf16)

        def gather(q, one):
            remote(
                proj.at[z, q], proj.at[z, q], send_sem.at[2], gather_recv.at[z], {"dp": one}
            ).start()

        @pl.when((layer == 0) | (x == q // 2))
        def _(q=q):
            for one in others[:0:-1]:
                gather(q, one)

        gather(q, others[0])

    @pl.when(layer == 1)
    def _():
        for one in train_swaps:
            one.start()

    @pl.when(stage < 2)
    def _():
        for b in range(2):
            train_project(2 + b)

    def bench_feats(slot):
        with jax.named_scope("bench_feats"):
            both = jnp.concatenate(
                [bench_outer(proj.at[slot, 2 * h], proj.at[slot, 2 * h + 1]) for h in range(2)],
                axis=1,
            ).astype(bf16)
            for p in range(width // 2):
                feats[slot, :, p * 128 : p * 128 + 128] = both[p]

    order = [others[0]] + others[:0:-1]

    def forward():
        for slot in order[1:]:
            half = proj.at[slot, pl.ds(2 * x, 2)]
            landed(half, gather_recv.at[slot])
            remote(half, half, send_sem.at[2], forward_recv.at[slot], {"tensor": other}).start()

    pl.when((layer == 1) & (z > 0))(forward)

    halves = []
    for b in range(2):
        with jax.named_scope("train_swap_wait"):
            train_swaps[b].wait_recv()
        with jax.named_scope("train_feats"):
            halves.append(train_outer((train_part[2 + b] + train_recv[b]).T))
    with jax.named_scope("train_store"):
        both = jnp.concatenate(halves, axis=1).astype(bf16)
        per_slot = columns // 128
        for p in range(width // 2):
            at = p % per_slot * 128
            t_send[p // per_slot, :, at : at + 128] = both[p]

    def t_copy(target, where):
        remote(t_send.at[target], t_all.at[me], send_sem.at[3], t_recv.at[z], where).start()

    for one in reversed(others):
        for column in range(2):
            t_copy(one * 2 + column, {"dp": one, "tensor": column})
    t_copy(z * 2 + other, {"tensor": other})
    pltpu.make_async_copy(t_send.at[me], t_all.at[me], t_recv.at[z]).start()
    pl.when((layer == 1) & (z == 0))(forward)
    bench_feats(z)

    for place, slot in enumerate(order):
        with jax.named_scope("gather_wait"):

            if place == 0:
                landed(proj.at[slot], gather_recv.at[slot])
            else:

                @pl.when(layer == 0)
                def _(slot=slot):
                    landed(proj.at[slot], gather_recv.at[slot])

                @pl.when(layer == 1)
                def _(slot=slot):
                    landed(proj.at[slot, pl.ds(0, 2)], forward_recv.at[slot])

        bench_feats(slot)

    with jax.named_scope("pre_wait"):
        pre_load.wait()
    with jax.named_scope("pre_dot"):
        bench_pre = jnp.dot(
            feats[...].reshape(n_dp * 16, feats.shape[2]), pre_v[...], preferred_element_type=f32
        )
        pre_high = bench_pre.astype(bf16)
        pre_low = (bench_pre - pre_high.astype(f32)).astype(bf16)
        pre_both = jnp.concatenate([pre_high, pre_low], axis=0)

    own = me * 2 + layer
    for at in range(n_dp):
        with jax.named_scope("t_wait"):
            landed(t_all.at[pl.ds(2 * at, 2)], t_recv.at[at])
        with jax.named_scope("score_dot"):
            held = t_all[2 * at : 2 * at + 2].reshape(32, columns)
            wide = lax.dot_general(held, pre_both, along, preferred_element_type=f32)
            partial_v[4 * at : 4 * at + 4] = (wide + pltpu.roll(wide, n_dp * 16, 1)).reshape(4, 8, 128)
        for column, core in ((other, 1 - layer), (other, layer), (x, 1 - layer)):
            remote(
                partial_v.at[4 * at + 2 * column + core], score_recv.at[own],
                send_sem.at[4], score_sem.at[0],
                {"dp": at, "tensor": column, "layer": core},
            ).start()
        mine = partial_v.at[4 * at + 2 * x + layer]

        @pl.when(z == at)
        def _():
            pltpu.make_async_copy(mine, score_recv.at[own], score_sem.at[0]).start()

        @pl.when(z != at)
        def _():
            remote(mine, score_recv.at[own], send_sem.at[4], score_sem.at[0], {"dp": at}).start()

    with jax.named_scope("score_wait"):
        landed(score_recv, score_sem.at[0])
    result = score_recv[0]
    for index in range(1, 2 * slots):
        result = result + score_recv[index]
    out[...] = result[:, : out.shape[1]] * scale

    with jax.named_scope("send_wait"):
        landed(bench_send, send_sem.at[0])
        landed(train_part.at[pl.ds(0, 2)], send_sem.at[1])
        landed(proj.at[pl.ds(0, n_dp - 1)], send_sem.at[2])
        landed(t_send.at[pl.ds(0, slots - 1)], send_sem.at[3])
        landed(partial_v.at[pl.ds(0, 2 * slots - 1)], send_sem.at[4])


def fused(train_inputs, train_grads, bench_inputs, bench_grads, answer_mask, factors, precond):
    f32, bf16 = jnp.float32, jnp.bfloat16
    _, train, length, shard = train_inputs.shape
    bench = bench_inputs.shape[1]
    n_dp = lax.axis_size("dp")
    slots = 2 * n_dp
    features, columns = precond.shape[1:]
    scale = 1.0 / math.sqrt(features * lax.axis_size("layer"))
    tile = 8 * length
    dma = pltpu.SemaphoreType.DMA
    anywhere = pl.BlockSpec(memory_space=pl.ANY)
    return pl.pallas_call(
        functools.partial(fused_kernel, (n_dp, scale)),
        out_shape=pltpu.VMEM((8, n_dp * bench), f32),
        in_specs=[anywhere] * 7,
        out_specs=pl.BlockSpec(memory_space=pltpu.VMEM),
        scratch_shapes=[
            pltpu.VMEM((4, 2, tile // 2, shard), bf16),
            pltpu.VMEM((4, 2, tile, shard), bf16),
            pltpu.VMEM((shard, 128), bf16),
            pltpu.VMEM((bench, length), jnp.int32),
            pltpu.VMEM((features, columns), bf16),
            pltpu.VMEM((4, tile // 2, 128), f32),
            pltpu.VMEM((4, tile // 2, 128), bf16),
            pltpu.VMEM((4, tile // 2, 128), bf16),
            pltpu.VMEM((4, tile, 128), f32),
            pltpu.VMEM((2, tile, 128), f32),
            pltpu.VMEM((n_dp, 4, 64, 128), bf16),
            pltpu.VMEM((n_dp, bench, features), bf16),
            pltpu.VMEM((slots, 16, columns), bf16),
            pltpu.VMEM((slots, 16, columns), bf16),
            pltpu.VMEM((2 * slots, 8, 128), f32),
            pltpu.VMEM((2 * slots, 8, 128), f32),
            dma((11,)),
            dma((6,)),
            dma((n_dp,)),
            dma((n_dp,)),
            dma((n_dp,)),
            dma((1,)),
            dma((5,)),
        ],
        compiler_params=pltpu.CompilerParams(
            collective_id=0, has_side_effects=True, vmem_limit_bytes=56 * 1024 * 1024
        ),
    )(
        train_inputs.reshape(train * length, shard),
        train_grads.reshape(train * length, shard),
        bench_inputs.reshape(bench * length, shard),
        bench_grads.reshape(bench * length, shard),
        answer_mask,
        factors[0],
        precond[0],
    )


def fits(shapes, sizes):
    train, bench, length, shard, half_width, features, columns, layers = shapes
    n_dp, n_tensor, n_layer = sizes
    return (
        n_tensor == 2 and n_layer == 2 and layers == 1 and half_width == 64 and length == 16
        and bench == 16 and train == 32 and n_dp == 4
        and shard % 256 == 0 and columns % 128 == 0 and features == 4096
        and features == 2 * n_dp * columns
    )


def local_any(*args):
    train_inputs, _, bench_inputs, _, _, factors, precond = args
    shapes = (
        train_inputs.shape[1], bench_inputs.shape[1], train_inputs.shape[2], train_inputs.shape[3],
        factors.shape[2] // 2, precond.shape[1], precond.shape[2], train_inputs.shape[0],
    )
    sizes = tuple(lax.axis_size(name) for name in ("dp", "tensor", "layer"))
    return fused(*args) if fits(shapes, sizes) else local(*args)


def solution(mesh):
    placed = (
        P("layer", ("groups", "dp"), None, "tensor"),
        P("layer", ("groups", "dp"), None, "tensor"),
        P("layer", ("groups", "dp"), None, "tensor"),
        P("layer", ("groups", "dp"), None, "tensor"),
        P(("groups", "dp"), None),
        P("layer", "tensor", None),
        P("layer", None, ("dp", "tensor")),
    )
    return jax.shard_map(
        local_any,
        mesh=mesh,
        in_specs=placed,
        out_specs=P(("groups", "dp", "tensor", "layer"), None),
        check_vma=False,
    )
```

```python
import functools
import math

import jax
import jax.numpy as jnp
from jax import lax
from jax.experimental import pallas as pl
from jax.experimental.pallas import tpu as pltpu
from jax.sharding import PartitionSpec as P

MESH = pl.DeviceIdType.MESH


def project(inputs_here, grads_here, factor):
    examples, length, shard_width = inputs_here.shape
    factor_width = factor.shape[1] // 2
    in_proj = jnp.dot(
        inputs_here.reshape(examples * length, shard_width),
        factor[:, :factor_width],
        preferred_element_type=jnp.float32,
    )
    out_proj = jnp.dot(
        grads_here.reshape(examples * length, shard_width),
        factor[:, factor_width:],
        preferred_element_type=jnp.float32,
    )
    return jnp.concatenate([in_proj, out_proj], axis=1)


def outer_features(token_rows, examples, length, factor_width):
    grouped = token_rows.reshape(examples, length, 2 * factor_width)
    outer = jnp.einsum(
        "esa,esb->eab",
        grouped[..., factor_width:],
        grouped[..., :factor_width],
        precision=lax.Precision.HIGHEST,
    ) / math.sqrt(length)
    return outer.reshape(examples, factor_width * factor_width).astype(jnp.bfloat16)


def local(train_inputs, train_grads, bench_inputs, bench_grads, answer_mask, factors, precond):
    factor = factors[0]
    factor_width = factor.shape[1] // 2
    length = train_inputs.shape[2]
    masked = bench_grads[0] * answer_mask.astype(jnp.bfloat16)[:, :, None]
    train_rows = project(train_inputs[0], train_grads[0], factor)
    bench_rows = project(bench_inputs[0], masked, factor)
    tensor_count = lax.axis_size("tensor")
    train_each = train_inputs.shape[1] // tensor_count
    bench_each = bench_inputs.shape[1] // tensor_count
    row_width = train_rows.shape[1]
    blocks = jnp.concatenate(
        [
            train_rows.reshape(tensor_count, train_each * length, row_width),
            bench_rows.reshape(tensor_count, bench_each * length, row_width),
        ],
        axis=1,
    ).reshape(-1, row_width)
    share_rows = blocks.shape[0] // tensor_count
    summed = lax.psum(blocks, "tensor")
    own_rows = lax.dynamic_slice_in_dim(
        summed, lax.axis_index("tensor") * share_rows, share_rows, 0
    )
    train_feats = outer_features(own_rows[: train_each * length], train_each, length, factor_width)
    bench_feats = outer_features(own_rows[train_each * length :], bench_each, length, factor_width)
    columns = precond[0]
    pre_cols = jnp.dot(
        lax.all_gather(bench_feats, ("dp", "tensor"), axis=0, tiled=True),
        columns,
        preferred_element_type=jnp.float32,
    ).astype(jnp.bfloat16)
    layer_total = lax.axis_size("layer") * train_inputs.shape[0]
    score_scale = 1.0 / math.sqrt(factor_width * factor_width * layer_total)
    whole_pre = lax.all_gather(pre_cols, ("dp", "tensor"), axis=1, tiled=True)
    partial_value = jnp.einsum(
        "ek,jk->ej", train_feats, whole_pre, preferred_element_type=jnp.float32
    )
    scores = lax.psum_scatter(partial_value, "layer", scatter_dimension=0, tiled=True)
    return scores * score_scale


def fused_kernel(
    dims,
    ti, tg, bi, bg, mask, fac, pre,
    out,
    bench_v, train_v, fac_v, mask_v, pre_v,
    bench_part, bench_send, bench_recv, train_part, train_recv,
    proj, feats, t_send, t_all, partial_v, score_recv,
    load_sem, swap_recv, gather_recv, forward_recv, t_recv, score_sem, send_sem, go_sem, pass_sem,
):
    n_dp, scale = dims
    f32, bf16 = jnp.float32, jnp.bfloat16
    z, x, layer = lax.axis_index("dp"), lax.axis_index("tensor"), lax.axis_index("layer")
    other = 1 - x
    me = z * 2 + x
    slots = 2 * n_dp
    length = mask.shape[1]
    shard = fac.shape[0]
    columns = pre_v.shape[1]
    width = 64
    tile = 8 * length
    piece = tile // 2
    along = (((1,), (1,)), ((), ()))

    def load(source, target, index):
        copy = pltpu.make_async_copy(source, target, load_sem.at[index])
        copy.start()
        return copy

    def rows_of(ref, index, rows):
        return ref.at[pl.ds(pl.multiple_of(index * rows, rows), rows), :]

    mask_load = load(mask, mask_v, 0)
    fac_load = load(fac, fac_v, 1)
    pieces = ((0, piece), (piece, piece), (tile, tile))
    for q, (start, rows) in enumerate(pieces):
        for i, ref in enumerate((bi, bg)):
            load(
                ref.at[pl.ds(start, rows), :],
                bench_v.at[start // tile, i, pl.ds(start % tile, rows)], 2 + q,
            )
    for b, index in enumerate((2 * other, 2 * other + 1, 2 * x, 2 * x + 1)):
        for i, ref in enumerate((ti, tg)):
            load(rows_of(ref, index, tile), train_v.at[b, i], 5 + b)
    pre_load = load(pre, pre_v, 9)

    def landed(ref, sem):
        pltpu.make_async_copy(ref, ref, sem).wait()

    near = jnp.where(2 * z < n_dp, z, n_dp - 1 - z)

    def line(i):
        place = jnp.where(near <= i, i + 1, i)
        return jnp.where(2 * z < n_dp, place, n_dp - 1 - place)

    others = [line(i) for i in range(n_dp - 1)]

    corner = (z == 0) & (x == 0)
    stage = jnp.where(
        layer == 0,
        jnp.where((z < 2) & (x == 0), 1, 0),
        jnp.where(z > 1, 0, jnp.where(corner, 2, 1)),
    )

    barrier = pltpu.get_barrier_semaphore()

    def greet(where):
        pl.semaphore_signal(barrier, inc=1, device_id=where, device_id_type=MESH)

    greet({"tensor": other})

    @pl.when(layer == 0)
    def _():
        greet({"layer": 1})

    @pl.when(layer == 1)
    def _():
        for one in others:
            greet({"dp": one})

    def enter():
        pl.semaphore_wait(barrier, jnp.where(layer == 0, 1, n_dp + 1))

        @pl.when(layer == 1)
        def _():
            for one in others:
                pl.semaphore_signal(go_sem, inc=1, device_id={"dp": one}, device_id_type=MESH)

    def remote(source, target, send, recv, where):
        return pltpu.make_async_remote_copy(
            source, target, send, recv, device_id=where, device_id_type=MESH
        )

    lane8 = lax.broadcasted_iota(jnp.int32, (8, tile), 1)
    row8 = lax.broadcasted_iota(jnp.int32, (8, tile), 0)
    root = 1.0 / math.sqrt(length)
    same = lane8 // length == row8
    block = jnp.where(same, root, 0.0)

    def project(ref):
        rows = ref.shape[1]
        both = jnp.dot(
            ref[...].reshape(2 * rows, shard), fac_v[...], preferred_element_type=f32
        )
        lane = lax.broadcasted_iota(jnp.int32, (rows, 128), 1)
        return jnp.where(lane < width, both[:rows], both[rows:])

    def spread(rows):
        whole = jnp.broadcast_to(rows[:, None, :], (width, 8, tile)) * block[None]
        pairs = whole.reshape(width // 2, 2, 8, tile)
        even = pairs[:, 0].reshape(width * 4, tile)
        odd = pairs[:, 1].reshape(width * 4, tile)
        return jnp.concatenate([even, odd], axis=1)

    def paired(rows):
        zero = jnp.zeros_like(rows)
        return jnp.concatenate(
            [jnp.concatenate([rows, zero], axis=1), jnp.concatenate([zero, rows], axis=1)], axis=0
        )

    def outer(left, right):
        return lax.dot_general(left, right, along, preferred_element_type=f32).reshape(
            width // 2, 8, 128
        )

    def bench_outer(ref):
        tokens = ref[...]
        return outer(spread(tokens[width:].astype(f32)).astype(bf16), paired(tokens[:width]))

    def train_outer(whole):
        left, right = spread(whole[width:]), paired(whole[:width])
        left_high, right_high = left.astype(bf16), right.astype(bf16)
        left_low = (left - left_high.astype(f32)).astype(bf16)
        right_low = (right - right_high.astype(f32)).astype(bf16)
        return outer(
            jnp.concatenate([left_high, left_low, left_high], axis=1),
            jnp.concatenate([right_high, right_high, right_low], axis=1),
        )

    with jax.named_scope("keep"):
        mask_load.wait()
        keeps = []
        lay = jnp.where(
            lax.broadcasted_iota(jnp.int32, (length, tile), 1) % length
            == lax.broadcasted_iota(jnp.int32, (length, tile), 0),
            1.0, 0.0,
        ).astype(bf16)
        for b in range(2):
            flags = mask_v[pl.ds(8 * b, 8), :].astype(f32).astype(bf16)
            tiled = jnp.dot(flags, lay, preferred_element_type=f32)
            masked = jnp.where(same, tiled, 0.0).astype(bf16)
            keeps.append(jnp.dot(jnp.ones((width, 8), bf16), masked, preferred_element_type=f32))

    def bench_rows(ref, q):
        start, rows = pieces[q]
        return ref.at[start // tile, pl.ds(start % tile, rows)]

    bench_swaps = [
        remote(
            bench_rows(bench_send, q), bench_rows(bench_recv, q),
            send_sem.at[0], swap_recv.at[q], {"tensor": other},
        )
        for q in range(3)
    ]
    train_swaps = [
        remote(
            train_part.at[b], train_recv.at[b], send_sem.at[1], swap_recv.at[3 + b],
            {"tensor": other},
        )
        for b in range(2)
    ]

    with jax.named_scope("fac_wait"):
        fac_load.wait()
    for q, (start, rows) in enumerate(pieces):
        held = bench_v.at[start // tile, :, pl.ds(start % tile, rows)]
        with jax.named_scope("bench_load_wait"):
            landed(held, load_sem.at[2 + q])
        with jax.named_scope("bench_project"):
            value = project(held)
            bench_rows(bench_part, q)[...] = value
            bench_rows(bench_send, q)[...] = value.astype(bf16)

        @pl.when(stage == 0)
        def _(q=q):
            if q == 0:
                enter()
            bench_swaps[q].start()

    @pl.when(stage == 1)
    def _():
        enter()
        for one in bench_swaps:
            one.start()

    def train_project(b):
        with jax.named_scope("train_load_wait"):
            landed(train_v.at[b], load_sem.at[5 + b])
        with jax.named_scope("train_project"):
            train_part[b] = project(train_v.at[b])

    for b in range(2):
        train_project(b)

        @pl.when((stage < 2) & (layer == 0))
        def _(b=b):
            train_swaps[b].start()

    @pl.when(stage == 2)
    def _():
        enter()
        for one in bench_swaps:
            one.start()

    @pl.when((stage == 2) & (layer == 0))
    def _():
        for one in train_swaps:
            one.start()

    @pl.when(corner)
    def _():
        for b in range(2):
            train_project(2 + b)

    @pl.when(layer == 1)
    def _():
        pl.semaphore_wait(go_sem, n_dp - 1)
        pl.semaphore_signal(go_sem, inc=1, device_id={"layer": 0}, device_id_type=MESH)

    for b in range(2):
        with jax.named_scope("bench_swap_wait"):
            for q in ((0, 1), (2,))[b]:
                bench_swaps[q].wait_recv()
        with jax.named_scope("bench_turn"):
            turned = (bench_part[b] + bench_recv[b].astype(f32)).T
            proj[z, b] = jnp.concatenate(
                [turned[:width], turned[width:] * keeps[b]], axis=0
            ).astype(bf16)

        if b == 0:

            @pl.when(layer == 0)
            def _():
                pl.semaphore_wait(go_sem, 1)
                pl.semaphore_signal(
                    pass_sem, inc=1, device_id={"tensor": other}, device_id_type=MESH
                )

        def gather(b, one):
            remote(
                proj.at[z, b], proj.at[z, b], send_sem.at[2], gather_recv.at[z], {"dp": one}
            ).start()

        @pl.when((layer == 0) | (x == b))
        def _(b=b):
            for one in others[:0:-1]:
                gather(b, one)

        gather(b, others[0])

    @pl.when(layer == 1)
    def _():
        for one in train_swaps:
            one.start()

    @pl.when(jnp.logical_not(corner))
    def _():
        for b in range(2):
            train_project(2 + b)

    def bench_feats(slot):
        with jax.named_scope("bench_feats"):
            both = jnp.concatenate(
                [bench_outer(proj.at[slot, 0]), bench_outer(proj.at[slot, 1])], axis=1
            ).astype(bf16)
            for p in range(width // 2):
                feats[slot, :, p * 128 : p * 128 + 128] = both[p]

    order = [others[0]] + others[:0:-1]

    def forward():
        for slot in order[1:]:
            half = proj.at[slot, x]
            landed(half, gather_recv.at[slot])
            remote(half, half, send_sem.at[2], forward_recv.at[slot], {"tensor": other}).start()

    pl.when((layer == 1) & (z > 0))(forward)

    halves = []
    for b in range(2):
        with jax.named_scope("train_swap_wait"):
            train_swaps[b].wait_recv()
        with jax.named_scope("train_feats"):
            halves.append(train_outer((train_part[2 + b] + train_recv[b]).T))
    with jax.named_scope("train_store"):
        both = jnp.concatenate(halves, axis=1).astype(bf16)
        per_slot = columns // 128
        for p in range(width // 2):
            at = p % per_slot * 128
            t_send[p // per_slot, :, at : at + 128] = both[p]

    def t_copy(target, where):
        remote(t_send.at[target], t_all.at[me], send_sem.at[3], t_recv.at[z], where).start()

    bench_feats(z)

    @pl.when(layer == 0)
    def _():
        pl.semaphore_wait(pass_sem, 1)

    for one in reversed(others):
        for column in range(2):
            t_copy(one * 2 + column, {"dp": one, "tensor": column})
    t_copy(z * 2 + other, {"tensor": other})
    pltpu.make_async_copy(t_send.at[me], t_all.at[me], t_recv.at[z]).start()
    pl.when((layer == 1) & (z == 0))(forward)

    for place, slot in enumerate(order):
        with jax.named_scope("gather_wait"):

            if place == 0:
                landed(proj.at[slot], gather_recv.at[slot])
            else:

                @pl.when(layer == 0)
                def _(slot=slot):
                    landed(proj.at[slot], gather_recv.at[slot])

                @pl.when(layer == 1)
                def _(slot=slot):
                    landed(proj.at[slot, 0], forward_recv.at[slot])

        bench_feats(slot)

    with jax.named_scope("pre_wait"):
        pre_load.wait()
    with jax.named_scope("pre_dot"):
        bench_pre = jnp.dot(
            feats[...].reshape(n_dp * 16, feats.shape[2]), pre_v[...], preferred_element_type=f32
        )
        pre_high = bench_pre.astype(bf16)
        pre_low = (bench_pre - pre_high.astype(f32)).astype(bf16)
        pre_both = jnp.concatenate([pre_high, pre_low], axis=0)

    own = me * 2 + layer
    low_lanes = lax.broadcasted_iota(jnp.int32, (32, 128), 1) < width
    half_rows = pl.ds(0, 4)
    landing = score_recv.at[own, half_rows]
    for at in range(n_dp):
        with jax.named_scope("t_wait"):
            landed(t_all.at[pl.ds(2 * at, 2)], t_recv.at[at])
        with jax.named_scope("score_dot"):
            held = t_all[2 * at : 2 * at + 2].reshape(32, columns)
            wide = lax.dot_general(held, pre_both, along, preferred_element_type=f32)
            both = wide + pltpu.roll(wide, n_dp * 16, 1)
            packed = jnp.where(low_lanes, both, pltpu.roll(both, 28, 0))
            partial_v[4 * at : 4 * at + 4] = packed.reshape(4, 8, 128)
        for column, core in ((other, 1 - layer), (other, layer), (x, 1 - layer)):
            remote(
                partial_v.at[4 * at + 2 * column + core, half_rows], landing,
                send_sem.at[4], score_sem.at[0],
                {"dp": at, "tensor": column, "layer": core},
            ).start()
        mine = partial_v.at[4 * at + 2 * x + layer, half_rows]

        @pl.when(z == at)
        def _():
            pltpu.make_async_copy(mine, landing, score_sem.at[0]).start()

        @pl.when(z != at)
        def _():
            remote(mine, landing, send_sem.at[4], score_sem.at[0], {"dp": at}).start()

    with jax.named_scope("score_wait"):
        landed(score_recv.at[pl.ds(0, slots)], score_sem.at[0])
    result = score_recv[0, :4, :]
    for index in range(1, 2 * slots):
        result = result + score_recv[index, :4, :]
    result = result * scale
    out[:4, :] = result[:, :width]
    out[4:, :] = result[:, width:]

    with jax.named_scope("send_wait"):
        landed(bench_send, send_sem.at[0])
        landed(train_part.at[pl.ds(0, 2)], send_sem.at[1])
        landed(proj.at[pl.ds(0, n_dp - 1)], send_sem.at[2])
        landed(t_send.at[pl.ds(0, slots - 1)], send_sem.at[3])
        landed(partial_v.at[pl.ds(0, 2 * slots - 1), half_rows], send_sem.at[4])


def fused(train_inputs, train_grads, bench_inputs, bench_grads, answer_mask, factors, precond):
    f32, bf16 = jnp.float32, jnp.bfloat16
    _, train, length, shard = train_inputs.shape
    bench = bench_inputs.shape[1]
    n_dp = lax.axis_size("dp")
    slots = 2 * n_dp
    features, columns = precond.shape[1:]
    scale = 1.0 / math.sqrt(features * lax.axis_size("layer"))
    tile = 8 * length
    dma = pltpu.SemaphoreType.DMA
    anywhere = pl.BlockSpec(memory_space=pl.ANY)
    return pl.pallas_call(
        functools.partial(fused_kernel, (n_dp, scale)),
        out_shape=pltpu.VMEM((8, n_dp * bench), f32),
        in_specs=[anywhere] * 7,
        out_specs=pl.BlockSpec(memory_space=pltpu.VMEM),
        scratch_shapes=[
            pltpu.VMEM((2, 2, tile, shard), bf16),
            pltpu.VMEM((4, 2, tile, shard), bf16),
            pltpu.VMEM((shard, 128), bf16),
            pltpu.VMEM((bench, length), jnp.int32),
            pltpu.VMEM((features, columns), bf16),
            pltpu.VMEM((2, tile, 128), f32),
            pltpu.VMEM((2, tile, 128), bf16),
            pltpu.VMEM((2, tile, 128), bf16),
            pltpu.VMEM((4, tile, 128), f32),
            pltpu.VMEM((2, tile, 128), f32),
            pltpu.VMEM((n_dp, 2, 128, 128), bf16),
            pltpu.VMEM((n_dp, bench, features), bf16),
            pltpu.VMEM((slots, 16, columns), bf16),
            pltpu.VMEM((slots, 16, columns), bf16),
            pltpu.VMEM((2 * slots, 8, 128), f32),
            pltpu.VMEM((2 * slots, 8, 128), f32),
            dma((10,)),
            dma((5,)),
            dma((n_dp,)),
            dma((n_dp,)),
            dma((n_dp,)),
            dma((1,)),
            dma((5,)),
            pltpu.SemaphoreType.REGULAR,
            pltpu.SemaphoreType.REGULAR,
        ],
        compiler_params=pltpu.CompilerParams(
            collective_id=0, has_side_effects=True, vmem_limit_bytes=56 * 1024 * 1024
        ),
    )(
        train_inputs.reshape(train * length, shard),
        train_grads.reshape(train * length, shard),
        bench_inputs.reshape(bench * length, shard),
        bench_grads.reshape(bench * length, shard),
        answer_mask,
        factors[0],
        precond[0],
    )


def fits(shapes, sizes):
    train, bench, length, shard, half_width, features, columns, layers = shapes
    n_dp, n_tensor, n_layer = sizes
    return (
        n_tensor == 2 and n_layer == 2 and layers == 1 and half_width == 64 and length == 16
        and bench == 16 and train == 32 and n_dp == 4
        and shard % 256 == 0 and columns % 128 == 0 and features == 4096
        and features == 2 * n_dp * columns
    )


def local_any(*args):
    train_inputs, _, bench_inputs, _, _, factors, precond = args
    shapes = (
        train_inputs.shape[1], bench_inputs.shape[1], train_inputs.shape[2], train_inputs.shape[3],
        factors.shape[2] // 2, precond.shape[1], precond.shape[2], train_inputs.shape[0],
    )
    sizes = tuple(lax.axis_size(name) for name in ("dp", "tensor", "layer"))
    return fused(*args) if fits(shapes, sizes) else local(*args)


def solution(mesh):
    placed = (
        P("layer", ("groups", "dp"), None, "tensor"),
        P("layer", ("groups", "dp"), None, "tensor"),
        P("layer", ("groups", "dp"), None, "tensor"),
        P("layer", ("groups", "dp"), None, "tensor"),
        P(("groups", "dp"), None),
        P("layer", "tensor", None),
        P("layer", None, ("dp", "tensor")),
    )
    return jax.shard_map(
        local_any,
        mesh=mesh,
        in_specs=placed,
        out_specs=P(("groups", "dp", "tensor", "layer"), None),
        check_vma=False,
    )
```

```python
import functools
import math

import jax
import jax.numpy as jnp
from jax import lax
from jax.experimental import pallas as pl
from jax.experimental.pallas import tpu as pltpu
from jax.sharding import PartitionSpec as P

MESH = pl.DeviceIdType.MESH


def project(inputs_here, grads_here, factor):
    examples, length, shard_width = inputs_here.shape
    factor_width = factor.shape[1] // 2
    in_proj = jnp.dot(
        inputs_here.reshape(examples * length, shard_width),
        factor[:, :factor_width],
        preferred_element_type=jnp.float32,
    )
    out_proj = jnp.dot(
        grads_here.reshape(examples * length, shard_width),
        factor[:, factor_width:],
        preferred_element_type=jnp.float32,
    )
    return jnp.concatenate([in_proj, out_proj], axis=1)


def outer_features(token_rows, examples, length, factor_width):
    grouped = token_rows.reshape(examples, length, 2 * factor_width)
    outer = jnp.einsum(
        "esa,esb->eab",
        grouped[..., factor_width:],
        grouped[..., :factor_width],
        precision=lax.Precision.HIGHEST,
    ) / math.sqrt(length)
    return outer.reshape(examples, factor_width * factor_width).astype(jnp.bfloat16)


def local(train_inputs, train_grads, bench_inputs, bench_grads, answer_mask, factors, precond):
    factor = factors[0]
    factor_width = factor.shape[1] // 2
    length = train_inputs.shape[2]
    masked = bench_grads[0] * answer_mask.astype(jnp.bfloat16)[:, :, None]
    train_rows = project(train_inputs[0], train_grads[0], factor)
    bench_rows = project(bench_inputs[0], masked, factor)
    tensor_count = lax.axis_size("tensor")
    train_each = train_inputs.shape[1] // tensor_count
    bench_each = bench_inputs.shape[1] // tensor_count
    row_width = train_rows.shape[1]
    blocks = jnp.concatenate(
        [
            train_rows.reshape(tensor_count, train_each * length, row_width),
            bench_rows.reshape(tensor_count, bench_each * length, row_width),
        ],
        axis=1,
    ).reshape(-1, row_width)
    share_rows = blocks.shape[0] // tensor_count
    summed = lax.psum(blocks, "tensor")
    own_rows = lax.dynamic_slice_in_dim(
        summed, lax.axis_index("tensor") * share_rows, share_rows, 0
    )
    train_feats = outer_features(own_rows[: train_each * length], train_each, length, factor_width)
    bench_feats = outer_features(own_rows[train_each * length :], bench_each, length, factor_width)
    columns = precond[0]
    pre_cols = jnp.dot(
        lax.all_gather(bench_feats, ("dp", "tensor"), axis=0, tiled=True),
        columns,
        preferred_element_type=jnp.float32,
    ).astype(jnp.bfloat16)
    layer_total = lax.axis_size("layer") * train_inputs.shape[0]
    score_scale = 1.0 / math.sqrt(factor_width * factor_width * layer_total)
    whole_pre = lax.all_gather(pre_cols, ("dp", "tensor"), axis=1, tiled=True)
    partial_value = jnp.einsum(
        "ek,jk->ej", train_feats, whole_pre, preferred_element_type=jnp.float32
    )
    scores = lax.psum_scatter(partial_value, "layer", scatter_dimension=0, tiled=True)
    return scores * score_scale


def fused_kernel(
    dims,
    ti, tg, bi, bg, mask, fac, pre,
    out,
    bench_v, train_v, fac_v, mask_v, pre_v,
    bench_part, bench_send, bench_recv, train_part, train_recv,
    proj, feats, t_send, t_all, partial_v, score_recv,
    load_sem, swap_recv, gather_recv, forward_recv, t_recv, score_sem, send_sem,
):
    n_dp, scale = dims
    f32, bf16 = jnp.float32, jnp.bfloat16
    z, x, layer = lax.axis_index("dp"), lax.axis_index("tensor"), lax.axis_index("layer")
    other = 1 - x
    me = z * 2 + x
    slots = 2 * n_dp
    length = mask.shape[1]
    shard = fac.shape[0]
    columns = pre_v.shape[1]
    width = 64
    tile = 8 * length
    piece = tile // 2
    along = (((1,), (1,)), ((), ()))

    def load(source, target, index):
        copy = pltpu.make_async_copy(source, target, load_sem.at[index])
        copy.start()
        return copy

    def rows_of(ref, index, rows):
        return ref.at[pl.ds(pl.multiple_of(index * rows, rows), rows), :]

    mask_load = load(mask, mask_v, 0)
    fac_load = load(fac, fac_v, 1)
    for q in range(4):
        for i, ref in enumerate((bi, bg)):
            load(rows_of(ref, q, piece), bench_v.at[q, i], 2 + q)
    for b, index in enumerate((2 * other, 2 * other + 1, 2 * x, 2 * x + 1)):
        for i, ref in enumerate((ti, tg)):
            load(rows_of(ref, index, tile), train_v.at[b, i], 6 + b)
    pre_load = load(pre, pre_v, 10)

    def landed(ref, sem):
        pltpu.make_async_copy(ref, ref, sem).wait()

    near = jnp.where(2 * z < n_dp, z, n_dp - 1 - z)

    def line(i):
        place = jnp.where(near <= i, i + 1, i)
        return jnp.where(2 * z < n_dp, place, n_dp - 1 - place)

    others = [line(i) for i in range(n_dp - 1)]

    stage = jnp.where(z > 1, 0, jnp.where(z + x > 0, 1, 2))

    barrier = pltpu.get_barrier_semaphore()
    for where in [{"dp": one} for one in others] + [{"tensor": other}, {"layer": 1 - layer}]:
        pl.semaphore_signal(barrier, inc=1, device_id=where, device_id_type=MESH)

    def remote(source, target, send, recv, where):
        return pltpu.make_async_remote_copy(
            source, target, send, recv, device_id=where, device_id_type=MESH
        )

    lane8 = lax.broadcasted_iota(jnp.int32, (8, tile), 1)
    row8 = lax.broadcasted_iota(jnp.int32, (8, tile), 0)
    root = 1.0 / math.sqrt(length)
    train_block = jnp.where(lane8 // length == row8, root, 0.0)
    bench_block = jnp.where((lane8 // length + 4) % 8 == row8, root, 0.0)

    def project(ref):
        rows = ref.shape[1]
        both = jnp.dot(
            ref[...].reshape(2 * rows, shard), fac_v[...], preferred_element_type=f32
        )
        lane = lax.broadcasted_iota(jnp.int32, (rows, 128), 1)
        return jnp.where(lane < width, both[:rows], both[rows:])

    def spread(rows, block):
        whole = jnp.broadcast_to(rows[:, None, :], (width, 8, tile)) * block[None]
        pairs = whole.reshape(width // 2, 2, 8, tile)
        even = pairs[:, 0].reshape(width * 4, tile)
        odd = pairs[:, 1].reshape(width * 4, tile)
        return jnp.concatenate([even, odd], axis=1)

    def paired(rows):
        zero = jnp.zeros_like(rows)
        return jnp.concatenate(
            [jnp.concatenate([rows, zero], axis=1), jnp.concatenate([zero, rows], axis=1)], axis=0
        )

    def outer(left, right):
        return lax.dot_general(left, right, along, preferred_element_type=f32).reshape(
            width // 2, 8, 128
        )

    def bench_outer(first, second):
        first, second = first[...].astype(f32), second[...].astype(f32)
        lane = lax.broadcasted_iota(jnp.int32, first.shape, 1)
        ins = jnp.where(lane < width, second, pltpu.roll(first, width, 1))
        outs = jnp.where(lane < width, pltpu.roll(second, width, 1), first)
        return outer(spread(outs, bench_block).astype(bf16), paired(ins).astype(bf16))

    def train_outer(whole):
        left, right = spread(whole[width:], train_block), paired(whole[:width])
        left_high, right_high = left.astype(bf16), right.astype(bf16)
        left_low = (left - left_high.astype(f32)).astype(bf16)
        right_low = (right - right_high.astype(f32)).astype(bf16)
        return outer(
            jnp.concatenate([left_high, left_low, left_high], axis=1),
            jnp.concatenate([right_high, right_high, right_low], axis=1),
        )

    with jax.named_scope("keep"):
        mask_load.wait()
        keeps = []
        lay = jnp.where(
            lax.broadcasted_iota(jnp.int32, (length, tile), 1) % length
            == lax.broadcasted_iota(jnp.int32, (length, tile), 0),
            1.0, 0.0,
        ).astype(bf16)
        for q in range(4):
            flags = mask_v[pl.ds(q // 2 * 8, 8), :].astype(f32).astype(bf16)
            tiled = jnp.dot(flags, lay, preferred_element_type=f32)
            wanted = (lane8 >= width) & ((lane8 - width) // length + 4 * (q % 2) == row8)
            masked = jnp.where(wanted, tiled, jnp.where((lane8 < width) & (row8 == 0), 1.0, 0.0))
            keeps.append(
                jnp.dot(jnp.ones((width, 8), bf16), masked.astype(bf16), preferred_element_type=f32)
            )

    bench_swaps = [
        remote(
            bench_send.at[q], bench_recv.at[q], send_sem.at[0], swap_recv.at[q], {"tensor": other}
        )
        for q in range(4)
    ]
    train_swaps = [
        remote(
            train_part.at[b], train_recv.at[b], send_sem.at[1], swap_recv.at[4 + b],
            {"tensor": other},
        )
        for b in range(2)
    ]

    with jax.named_scope("fac_wait"):
        fac_load.wait()
    for q in range(4):
        with jax.named_scope("bench_load_wait"):
            landed(bench_v.at[q], load_sem.at[2 + q])
        with jax.named_scope("bench_project"):
            value = project(bench_v.at[q])
            bench_part[q] = value
            bench_send[q] = value.astype(bf16)

        @pl.when(stage == 0)
        def _(q=q):
            if q == 0:
                pl.semaphore_wait(barrier, n_dp + 1)
            bench_swaps[q].start()

    @pl.when(stage == 1)
    def _():
        pl.semaphore_wait(barrier, n_dp + 1)
        for one in bench_swaps:
            one.start()

    def train_project(b):
        with jax.named_scope("train_load_wait"):
            landed(train_v.at[b], load_sem.at[6 + b])
        with jax.named_scope("train_project"):
            train_part[b] = project(train_v.at[b])

    for b in range(2):
        train_project(b)

        @pl.when((stage < 2) & (layer == 0))
        def _(b=b):
            train_swaps[b].start()

    @pl.when(stage == 2)
    def _():
        pl.semaphore_wait(barrier, n_dp + 1)
        for one in bench_swaps:
            one.start()

    @pl.when((stage == 2) & (layer == 0))
    def _():
        for one in train_swaps:
            one.start()

    @pl.when(stage == 2)
    def _():
        for b in range(2):
            train_project(2 + b)

    for q in range(4):
        with jax.named_scope("bench_swap_wait"):
            bench_swaps[q].wait_recv()
        with jax.named_scope("bench_turn"):
            turned = (bench_part[q] + bench_recv[q].astype(f32)).T
            proj[z, q] = (
                jnp.concatenate([turned[:width], turned[width:]], axis=1) * keeps[q]
            ).astype(bf16)

        def gather(q, one):
            remote(
                proj.at[z, q], proj.at[z, q], send_sem.at[2], gather_recv.at[z], {"dp": one}
            ).start()

        @pl.when((layer == 0) | (x == q // 2))
        def _(q=q):
            for one in others[:0:-1]:
                gather(q, one)

        gather(q, others[0])

    @pl.when(layer == 1)
    def _():
        for one in train_swaps:
            one.start()

    @pl.when(stage < 2)
    def _():
        for b in range(2):
            train_project(2 + b)

    def bench_feats(slot):
        with jax.named_scope("bench_feats"):
            both = jnp.concatenate(
                [bench_outer(proj.at[slot, 2 * h], proj.at[slot, 2 * h + 1]) for h in range(2)],
                axis=1,
            ).astype(bf16)
            for p in range(width // 2):
                feats[slot, :, p * 128 : p * 128 + 128] = both[p]

    order = [others[0]] + others[:0:-1]

    def forward():
        for slot in order[1:]:
            half = proj.at[slot, pl.ds(2 * x, 2)]
            landed(half, gather_recv.at[slot])
            remote(half, half, send_sem.at[2], forward_recv.at[slot], {"tensor": other}).start()

    pl.when((layer == 1) & (z > 0))(forward)

    halves = []
    for b in range(2):
        with jax.named_scope("train_swap_wait"):
            train_swaps[b].wait_recv()
        with jax.named_scope("train_feats"):
            halves.append(train_outer((train_part[2 + b] + train_recv[b]).T))
    with jax.named_scope("train_store"):
        both = jnp.concatenate(halves, axis=1).astype(bf16)
        per_slot = columns // 128
        for p in range(width // 2):
            at = p % per_slot * 128
            t_send[p // per_slot, :, at : at + 128] = both[p]

    def t_copy(target, where):
        remote(t_send.at[target], t_all.at[me], send_sem.at[3], t_recv.at[z], where).start()

    for one in reversed(others):
        for column in range(2):
            t_copy(one * 2 + column, {"dp": one, "tensor": column})
    t_copy(z * 2 + other, {"tensor": other})
    pltpu.make_async_copy(t_send.at[me], t_all.at[me], t_recv.at[z]).start()
    pl.when((layer == 1) & (z == 0))(forward)
    bench_feats(z)

    for place, slot in enumerate(order):
        with jax.named_scope("gather_wait"):

            if place == 0:
                landed(proj.at[slot], gather_recv.at[slot])
            else:

                @pl.when(layer == 0)
                def _(slot=slot):
                    landed(proj.at[slot], gather_recv.at[slot])

                @pl.when(layer == 1)
                def _(slot=slot):
                    landed(proj.at[slot, pl.ds(0, 2)], forward_recv.at[slot])

        bench_feats(slot)

    with jax.named_scope("pre_wait"):
        pre_load.wait()
    with jax.named_scope("pre_dot"):
        bench_pre = jnp.dot(
            feats[...].reshape(n_dp * 16, feats.shape[2]), pre_v[...], preferred_element_type=f32
        )
        pre_high = bench_pre.astype(bf16)
        pre_low = (bench_pre - pre_high.astype(f32)).astype(bf16)
        pre_both = jnp.concatenate([pre_high, pre_low], axis=0)

    own = me * 2 + layer
    low_lanes = lax.broadcasted_iota(jnp.int32, (32, 128), 1) < width
    half_rows = pl.ds(0, 4)
    landing = score_recv.at[own, half_rows]
    for at in range(n_dp):
        with jax.named_scope("t_wait"):
            landed(t_all.at[pl.ds(2 * at, 2)], t_recv.at[at])
        with jax.named_scope("score_dot"):
            held = t_all[2 * at : 2 * at + 2].reshape(32, columns)
            wide = lax.dot_general(held, pre_both, along, preferred_element_type=f32)
            both = wide + pltpu.roll(wide, n_dp * 16, 1)
            packed = jnp.where(low_lanes, both, pltpu.roll(both, 28, 0))
            partial_v[4 * at : 4 * at + 4] = packed.reshape(4, 8, 128)
        for column, core in ((other, 1 - layer), (other, layer), (x, 1 - layer)):
            remote(
                partial_v.at[4 * at + 2 * column + core, half_rows], landing,
                send_sem.at[4], score_sem.at[0],
                {"dp": at, "tensor": column, "layer": core},
            ).start()
        mine = partial_v.at[4 * at + 2 * x + layer, half_rows]

        @pl.when(z == at)
        def _():
            pltpu.make_async_copy(mine, landing, score_sem.at[0]).start()

        @pl.when(z != at)
        def _():
            remote(mine, landing, send_sem.at[4], score_sem.at[0], {"dp": at}).start()

    with jax.named_scope("score_wait"):
        landed(score_recv.at[pl.ds(0, slots)], score_sem.at[0])
    result = score_recv[0, :4, :]
    for index in range(1, 2 * slots):
        result = result + score_recv[index, :4, :]
    result = result * scale
    out[:4, :] = result[:, :width]
    out[4:, :] = result[:, width:]

    with jax.named_scope("send_wait"):
        landed(bench_send, send_sem.at[0])
        landed(train_part.at[pl.ds(0, 2)], send_sem.at[1])
        landed(proj.at[pl.ds(0, n_dp - 1)], send_sem.at[2])
        landed(t_send.at[pl.ds(0, slots - 1)], send_sem.at[3])
        landed(partial_v.at[pl.ds(0, 2 * slots - 1), half_rows], send_sem.at[4])


def fused(train_inputs, train_grads, bench_inputs, bench_grads, answer_mask, factors, precond):
    f32, bf16 = jnp.float32, jnp.bfloat16
    _, train, length, shard = train_inputs.shape
    bench = bench_inputs.shape[1]
    n_dp = lax.axis_size("dp")
    slots = 2 * n_dp
    features, columns = precond.shape[1:]
    scale = 1.0 / math.sqrt(features * lax.axis_size("layer"))
    tile = 8 * length
    dma = pltpu.SemaphoreType.DMA
    anywhere = pl.BlockSpec(memory_space=pl.ANY)
    return pl.pallas_call(
        functools.partial(fused_kernel, (n_dp, scale)),
        out_shape=pltpu.VMEM((8, n_dp * bench), f32),
        in_specs=[anywhere] * 7,
        out_specs=pl.BlockSpec(memory_space=pltpu.VMEM),
        scratch_shapes=[
            pltpu.VMEM((4, 2, tile // 2, shard), bf16),
            pltpu.VMEM((4, 2, tile, shard), bf16),
            pltpu.VMEM((shard, 128), bf16),
            pltpu.VMEM((bench, length), jnp.int32),
            pltpu.VMEM((features, columns), bf16),
            pltpu.VMEM((4, tile // 2, 128), f32),
            pltpu.VMEM((4, tile // 2, 128), bf16),
            pltpu.VMEM((4, tile // 2, 128), bf16),
            pltpu.VMEM((4, tile, 128), f32),
            pltpu.VMEM((2, tile, 128), f32),
            pltpu.VMEM((n_dp, 4, 64, 128), bf16),
            pltpu.VMEM((n_dp, bench, features), bf16),
            pltpu.VMEM((slots, 16, columns), bf16),
            pltpu.VMEM((slots, 16, columns), bf16),
            pltpu.VMEM((2 * slots, 8, 128), f32),
            pltpu.VMEM((2 * slots, 8, 128), f32),
            dma((11,)),
            dma((6,)),
            dma((n_dp,)),
            dma((n_dp,)),
            dma((n_dp,)),
            dma((1,)),
            dma((5,)),
        ],
        compiler_params=pltpu.CompilerParams(
            collective_id=0, has_side_effects=True, vmem_limit_bytes=56 * 1024 * 1024
        ),
    )(
        train_inputs.reshape(train * length, shard),
        train_grads.reshape(train * length, shard),
        bench_inputs.reshape(bench * length, shard),
        bench_grads.reshape(bench * length, shard),
        answer_mask,
        factors[0],
        precond[0],
    )


def fits(shapes, sizes):
    train, bench, length, shard, half_width, features, columns, layers = shapes
    n_dp, n_tensor, n_layer = sizes
    return (
        n_tensor == 2 and n_layer == 2 and layers == 1 and half_width == 64 and length == 16
        and bench == 16 and train == 32 and n_dp == 4
        and shard % 256 == 0 and columns % 128 == 0 and features == 4096
        and features == 2 * n_dp * columns
    )


def local_any(*args):
    train_inputs, _, bench_inputs, _, _, factors, precond = args
    shapes = (
        train_inputs.shape[1], bench_inputs.shape[1], train_inputs.shape[2], train_inputs.shape[3],
        factors.shape[2] // 2, precond.shape[1], precond.shape[2], train_inputs.shape[0],
    )
    sizes = tuple(lax.axis_size(name) for name in ("dp", "tensor", "layer"))
    return fused(*args) if fits(shapes, sizes) else local(*args)


def solution(mesh):
    placed = (
        P("layer", ("groups", "dp"), None, "tensor"),
        P("layer", ("groups", "dp"), None, "tensor"),
        P("layer", ("groups", "dp"), None, "tensor"),
        P("layer", ("groups", "dp"), None, "tensor"),
        P(("groups", "dp"), None),
        P("layer", "tensor", None),
        P("layer", None, ("dp", "tensor")),
    )
    return jax.shard_map(
        local_any,
        mesh=mesh,
        in_specs=placed,
        out_specs=P(("groups", "dp", "tensor", "layer"), None),
        check_vma=False,
    )
```

```python
import functools
import math

import jax
import jax.numpy as jnp
from jax import lax
from jax.experimental import pallas as pl
from jax.experimental.pallas import tpu as pltpu
from jax.sharding import PartitionSpec as P

MESH = pl.DeviceIdType.MESH


def project(inputs_here, grads_here, factor):
    examples, length, shard_width = inputs_here.shape
    factor_width = factor.shape[1] // 2
    in_proj = jnp.dot(
        inputs_here.reshape(examples * length, shard_width),
        factor[:, :factor_width],
        preferred_element_type=jnp.float32,
    )
    out_proj = jnp.dot(
        grads_here.reshape(examples * length, shard_width),
        factor[:, factor_width:],
        preferred_element_type=jnp.float32,
    )
    return jnp.concatenate([in_proj, out_proj], axis=1)


def outer_features(token_rows, examples, length, factor_width):
    grouped = token_rows.reshape(examples, length, 2 * factor_width)
    outer = jnp.einsum(
        "esa,esb->eab",
        grouped[..., factor_width:],
        grouped[..., :factor_width],
        precision=lax.Precision.HIGHEST,
    ) / math.sqrt(length)
    return outer.reshape(examples, factor_width * factor_width).astype(jnp.bfloat16)


def local(train_inputs, train_grads, bench_inputs, bench_grads, answer_mask, factors, precond):
    factor = factors[0]
    factor_width = factor.shape[1] // 2
    length = train_inputs.shape[2]
    masked = bench_grads[0] * answer_mask.astype(jnp.bfloat16)[:, :, None]
    train_rows = project(train_inputs[0], train_grads[0], factor)
    bench_rows = project(bench_inputs[0], masked, factor)
    tensor_count = lax.axis_size("tensor")
    train_each = train_inputs.shape[1] // tensor_count
    bench_each = bench_inputs.shape[1] // tensor_count
    row_width = train_rows.shape[1]
    blocks = jnp.concatenate(
        [
            train_rows.reshape(tensor_count, train_each * length, row_width),
            bench_rows.reshape(tensor_count, bench_each * length, row_width),
        ],
        axis=1,
    ).reshape(-1, row_width)
    share_rows = blocks.shape[0] // tensor_count
    summed = lax.psum(blocks, "tensor")
    own_rows = lax.dynamic_slice_in_dim(
        summed, lax.axis_index("tensor") * share_rows, share_rows, 0
    )
    train_feats = outer_features(own_rows[: train_each * length], train_each, length, factor_width)
    bench_feats = outer_features(own_rows[train_each * length :], bench_each, length, factor_width)
    columns = precond[0]
    pre_cols = jnp.dot(
        lax.all_gather(bench_feats, ("dp", "tensor"), axis=0, tiled=True),
        columns,
        preferred_element_type=jnp.float32,
    ).astype(jnp.bfloat16)
    layer_total = lax.axis_size("layer") * train_inputs.shape[0]
    score_scale = 1.0 / math.sqrt(factor_width * factor_width * layer_total)
    whole_pre = lax.all_gather(pre_cols, ("dp", "tensor"), axis=1, tiled=True)
    partial_value = jnp.einsum(
        "ek,jk->ej", train_feats, whole_pre, preferred_element_type=jnp.float32
    )
    scores = lax.psum_scatter(partial_value, "layer", scatter_dimension=0, tiled=True)
    return scores * score_scale


def fused_kernel(
    dims,
    ti, tg, bi, bg, mask, fac, pre,
    out,
    bench_v, train_v, fac_v, mask_v, pre_v,
    bench_part, bench_send, bench_recv, train_part, train_recv,
    proj, feats, t_send, t_all, partial_v, score_recv,
    load_sem, swap_recv, gather_recv, t_recv, score_sem, send_sem,
):
    n_dp, scale = dims
    f32, bf16 = jnp.float32, jnp.bfloat16
    z, x, layer = lax.axis_index("dp"), lax.axis_index("tensor"), lax.axis_index("layer")
    other = 1 - x
    me = z * 2 + x
    slots = 2 * n_dp
    length = mask.shape[1]
    shard = fac.shape[0]
    columns = pre_v.shape[1]
    width = 64
    tile = 8 * length
    piece = tile // 2
    along = (((1,), (1,)), ((), ()))

    def load(source, target, index):
        copy = pltpu.make_async_copy(source, target, load_sem.at[index])
        copy.start()
        return copy

    def rows_of(ref, index, rows):
        return ref.at[pl.ds(pl.multiple_of(index * rows, rows), rows), :]

    mask_load = load(mask, mask_v, 0)
    fac_load = load(fac, fac_v, 1)
    for q in range(4):
        for i, ref in enumerate((bi, bg)):
            load(rows_of(ref, q, piece), bench_v.at[q, i], 2 + q)
    for b, index in enumerate((2 * other, 2 * other + 1, 2 * x, 2 * x + 1)):
        for i, ref in enumerate((ti, tg)):
            load(rows_of(ref, index, tile), train_v.at[b, i], 6 + min(b, 2))
    pre_load = load(pre, pre_v, 9)

    def landed(ref, sem):
        pltpu.make_async_copy(ref, ref, sem).wait()

    near = jnp.where(2 * z < n_dp, z, n_dp - 1 - z)

    def line(i):
        place = jnp.where(near <= i, i + 1, i)
        return jnp.where(2 * z < n_dp, place, n_dp - 1 - place)

    others = [line(i) for i in range(n_dp - 1)]

    stage = jnp.where(z > 1, 0, jnp.where(z + x > 0, 1, 2))

    barrier = pltpu.get_barrier_semaphore()
    for where in [{"dp": one} for one in others] + [{"tensor": other}, {"layer": 1 - layer}]:
        pl.semaphore_signal(barrier, inc=1, device_id=where, device_id_type=MESH)

    def remote(source, target, send, recv, where):
        return pltpu.make_async_remote_copy(
            source, target, send, recv, device_id=where, device_id_type=MESH
        )

    lane8 = lax.broadcasted_iota(jnp.int32, (8, tile), 1)
    row8 = lax.broadcasted_iota(jnp.int32, (8, tile), 0)
    root = 1.0 / math.sqrt(length)
    train_block = jnp.where(lane8 // length == row8, root, 0.0)
    bench_block = jnp.where((lane8 // length + 4) % 8 == row8, root, 0.0)

    def project(ref):
        rows = ref.shape[1]
        both = jnp.dot(
            ref[...].reshape(2 * rows, shard), fac_v[...], preferred_element_type=f32
        )
        lane = lax.broadcasted_iota(jnp.int32, (rows, 128), 1)
        return jnp.where(lane < width, both[:rows], both[rows:])

    def spread(rows, block):
        whole = jnp.broadcast_to(rows[:, None, :], (width, 8, tile)) * block[None]
        pairs = whole.reshape(width // 2, 2, 8, tile)
        even = pairs[:, 0].reshape(width * 4, tile)
        odd = pairs[:, 1].reshape(width * 4, tile)
        return jnp.concatenate([even, odd], axis=1)

    def paired(rows):
        zero = jnp.zeros_like(rows)
        return jnp.concatenate(
            [jnp.concatenate([rows, zero], axis=1), jnp.concatenate([zero, rows], axis=1)], axis=0
        )

    def outer(left, right):
        return lax.dot_general(left, right, along, preferred_element_type=f32).reshape(
            width // 2, 8, 128
        )

    def bench_outer(first, second):
        first, second = first[...].astype(f32), second[...].astype(f32)
        lane = lax.broadcasted_iota(jnp.int32, first.shape, 1)
        ins = jnp.where(lane < width, second, pltpu.roll(first, width, 1))
        outs = jnp.where(lane < width, pltpu.roll(second, width, 1), first)
        return outer(spread(outs, bench_block).astype(bf16), paired(ins).astype(bf16))

    def train_outer(whole):
        left, right = spread(whole[width:], train_block), paired(whole[:width])
        left_high, right_high = left.astype(bf16), right.astype(bf16)
        left_low = (left - left_high.astype(f32)).astype(bf16)
        right_low = (right - right_high.astype(f32)).astype(bf16)
        return outer(
            jnp.concatenate([left_high, left_low, left_high], axis=1),
            jnp.concatenate([right_high, right_high, right_low], axis=1),
        )

    with jax.named_scope("keep"):
        mask_load.wait()
        keeps = []
        lay = jnp.where(
            lax.broadcasted_iota(jnp.int32, (length, tile), 1) % length
            == lax.broadcasted_iota(jnp.int32, (length, tile), 0),
            1.0, 0.0,
        ).astype(bf16)
        for q in range(4):
            flags = mask_v[pl.ds(q // 2 * 8, 8), :].astype(f32).astype(bf16)
            tiled = jnp.dot(flags, lay, preferred_element_type=f32)
            wanted = (lane8 >= width) & ((lane8 - width) // length + 4 * (q % 2) == row8)
            masked = jnp.where(wanted, tiled, jnp.where((lane8 < width) & (row8 == 0), 1.0, 0.0))
            keeps.append(
                jnp.dot(jnp.ones((width, 8), bf16), masked.astype(bf16), preferred_element_type=f32)
            )

    bench_swaps = [
        remote(
            bench_send.at[q], bench_recv.at[q], send_sem.at[0], swap_recv.at[q], {"tensor": other}
        )
        for q in range(4)
    ]
    train_swaps = [
        remote(
            train_part.at[b], train_recv.at[b], send_sem.at[0], swap_recv.at[4 + b],
            {"tensor": other},
        )
        for b in range(2)
    ]

    with jax.named_scope("fac_wait"):
        fac_load.wait()
    for q in range(4):
        with jax.named_scope("bench_load_wait"):
            landed(bench_v.at[q], load_sem.at[2 + q])
        with jax.named_scope("bench_project"):
            value = project(bench_v.at[q])
            bench_part[q] = value
            bench_send[q] = value.astype(bf16)

        @pl.when(stage == 0)
        def _(q=q):
            if q == 0:
                pl.semaphore_wait(barrier, n_dp + 1)
            bench_swaps[q].start()

    @pl.when(stage == 1)
    def _():
        pl.semaphore_wait(barrier, n_dp + 1)
        for one in bench_swaps:
            one.start()

    def train_project(b):
        with jax.named_scope("train_load_wait"):
            if b < 2:
                landed(train_v.at[b], load_sem.at[6 + b])
            elif b == 2:
                landed(train_v.at[pl.ds(2, 2)], load_sem.at[8])
        with jax.named_scope("train_project"):
            train_part[b] = project(train_v.at[b])

    for b in range(2):
        train_project(b)

        @pl.when((stage < 2) & (layer == 0))
        def _(b=b):
            train_swaps[b].start()

    @pl.when(stage == 2)
    def _():
        pl.semaphore_wait(barrier, n_dp + 1)
        for one in bench_swaps:
            one.start()

    @pl.when((stage == 2) & (layer == 0))
    def _():
        for one in train_swaps:
            one.start()

    @pl.when(stage == 2)
    def _():
        for b in range(2):
            train_project(2 + b)

    for q in range(4):
        with jax.named_scope("bench_swap_wait"):
            bench_swaps[q].wait_recv()
        with jax.named_scope("bench_turn"):
            turned = (bench_part[q] + bench_recv[q].astype(f32)).T
            proj[z, q] = (
                jnp.concatenate([turned[:width], turned[width:]], axis=1) * keeps[q]
            ).astype(bf16)

        def gather(q, one):
            remote(
                proj.at[z, q], proj.at[z, q], send_sem.at[0], gather_recv.at[z], {"dp": one}
            ).start()

        @pl.when((layer == 0) | (x == q // 2))
        def _(q=q):
            for one in others[:0:-1]:
                gather(q, one)

        gather(q, others[0])

    @pl.when(layer == 1)
    def _():
        for one in train_swaps:
            one.start()

    @pl.when(stage < 2)
    def _():
        for b in range(2):
            train_project(2 + b)

    def bench_feats(slot):
        with jax.named_scope("bench_feats"):
            both = jnp.concatenate(
                [bench_outer(proj.at[slot, 2 * h], proj.at[slot, 2 * h + 1]) for h in range(2)],
                axis=1,
            ).astype(bf16)
            for p in range(width // 2):
                feats[slot, :, p * 128 : p * 128 + 128] = both[p]

    order = [others[0]] + others[:0:-1]

    passed = [z, n_dp]

    def forward():
        for index, slot in enumerate(order[1:]):
            half = proj.at[slot, pl.ds(2 * x, 2)]
            landed(half, gather_recv.at[slot])
            remote(half, half, send_sem.at[0], gather_recv.at[passed[index]], {"tensor": other}).start()

    pl.when((layer == 1) & (z > 0))(forward)

    halves = []
    for b in range(2):
        with jax.named_scope("train_swap_wait"):
            train_swaps[b].wait_recv()
        with jax.named_scope("train_feats"):
            halves.append(train_outer((train_part[2 + b] + train_recv[b]).T))
    with jax.named_scope("train_store"):
        both = jnp.concatenate(halves, axis=1).astype(bf16)
        per_slot = columns // 128
        for p in range(width // 2):
            at = p % per_slot * 128
            t_send[p // per_slot, :, at : at + 128] = both[p]

    def t_copy(target, where):
        remote(t_send.at[target], t_all.at[me], send_sem.at[1], t_recv.at[z], where).start()

    for one in reversed(others):
        for column in range(2):
            t_copy(one * 2 + column, {"dp": one, "tensor": column})
    t_copy(z * 2 + other, {"tensor": other})
    pltpu.make_async_copy(t_send.at[me], t_all.at[me], t_recv.at[z]).start()
    pl.when((layer == 1) & (z == 0))(forward)
    bench_feats(z)

    for place, slot in enumerate(order):
        with jax.named_scope("gather_wait"):

            if place == 0:
                landed(proj.at[slot], gather_recv.at[slot])
            else:

                @pl.when(layer == 0)
                def _(slot=slot):
                    landed(proj.at[slot], gather_recv.at[slot])

                @pl.when(layer == 1)
                def _(slot=slot, place=place):
                    landed(proj.at[slot, pl.ds(0, 2)], gather_recv.at[passed[place - 1]])

        bench_feats(slot)

    with jax.named_scope("pre_wait"):
        pre_load.wait()
    with jax.named_scope("pre_dot"):
        bench_pre = jnp.dot(
            feats[...].reshape(n_dp * 16, feats.shape[2]), pre_v[...], preferred_element_type=f32
        )
        pre_high = bench_pre.astype(bf16)
        pre_low = (bench_pre - pre_high.astype(f32)).astype(bf16)
        pre_both = jnp.concatenate([pre_high, pre_low], axis=0)

    own = me * 2 + layer
    for at in range(n_dp):
        with jax.named_scope("t_wait"):
            landed(t_all.at[pl.ds(2 * at, 2)], t_recv.at[at])
        with jax.named_scope("score_dot"):
            held = t_all[2 * at : 2 * at + 2].reshape(32, columns)
            wide = lax.dot_general(held, pre_both, along, preferred_element_type=f32)
            partial_v[4 * at : 4 * at + 4] = (wide + pltpu.roll(wide, n_dp * 16, 1)).reshape(4, 8, 128)
        for column, core in ((other, 1 - layer), (other, layer), (x, 1 - layer)):
            remote(
                partial_v.at[4 * at + 2 * column + core], score_recv.at[own],
                send_sem.at[2], score_sem.at[0],
                {"dp": at, "tensor": column, "layer": core},
            ).start()
        mine = partial_v.at[4 * at + 2 * x + layer]

        @pl.when(z == at)
        def _():
            pltpu.make_async_copy(mine, score_recv.at[own], score_sem.at[0]).start()

        @pl.when(z != at)
        def _():
            remote(mine, score_recv.at[own], send_sem.at[2], score_sem.at[0], {"dp": at}).start()

    with jax.named_scope("score_wait"):
        landed(score_recv, score_sem.at[0])
    result = score_recv[0]
    for index in range(1, 2 * slots):
        result = result + score_recv[index]
    out[...] = result[:, : out.shape[1]] * scale

    with jax.named_scope("send_wait"):
        landed(train_v.at[0, 0, pl.ds(0, 3 * tile // 8)], send_sem.at[0])
        landed(t_send.at[pl.ds(0, slots - 1)], send_sem.at[1])
        landed(partial_v.at[pl.ds(0, 2 * slots - 1)], send_sem.at[2])


def fused(train_inputs, train_grads, bench_inputs, bench_grads, answer_mask, factors, precond):
    f32, bf16 = jnp.float32, jnp.bfloat16
    _, train, length, shard = train_inputs.shape
    bench = bench_inputs.shape[1]
    n_dp = lax.axis_size("dp")
    slots = 2 * n_dp
    features, columns = precond.shape[1:]
    scale = 1.0 / math.sqrt(features * lax.axis_size("layer"))
    tile = 8 * length
    dma = pltpu.SemaphoreType.DMA
    anywhere = pl.BlockSpec(memory_space=pl.ANY)
    return pl.pallas_call(
        functools.partial(fused_kernel, (n_dp, scale)),
        out_shape=pltpu.VMEM((8, n_dp * bench), f32),
        in_specs=[anywhere] * 7,
        out_specs=pl.BlockSpec(memory_space=pltpu.VMEM),
        scratch_shapes=[
            pltpu.VMEM((4, 2, tile // 2, shard), bf16),
            pltpu.VMEM((4, 2, tile, shard), bf16),
            pltpu.VMEM((shard, 128), bf16),
            pltpu.VMEM((bench, length), jnp.int32),
            pltpu.VMEM((features, columns), bf16),
            pltpu.VMEM((4, tile // 2, 128), f32),
            pltpu.VMEM((4, tile // 2, 128), bf16),
            pltpu.VMEM((4, tile // 2, 128), bf16),
            pltpu.VMEM((4, tile, 128), f32),
            pltpu.VMEM((2, tile, 128), f32),
            pltpu.VMEM((n_dp, 4, 64, 128), bf16),
            pltpu.VMEM((n_dp, bench, features), bf16),
            pltpu.VMEM((slots, 16, columns), bf16),
            pltpu.VMEM((slots, 16, columns), bf16),
            pltpu.VMEM((2 * slots, 8, 128), f32),
            pltpu.VMEM((2 * slots, 8, 128), f32),
            dma((10,)),
            dma((6,)),
            dma((n_dp + 1,)),
            dma((n_dp,)),
            dma((1,)),
            dma((3,)),
        ],
        compiler_params=pltpu.CompilerParams(
            collective_id=0, has_side_effects=True, vmem_limit_bytes=56 * 1024 * 1024
        ),
    )(
        train_inputs.reshape(train * length, shard),
        train_grads.reshape(train * length, shard),
        bench_inputs.reshape(bench * length, shard),
        bench_grads.reshape(bench * length, shard),
        answer_mask,
        factors[0],
        precond[0],
    )


def fits(shapes, sizes):
    train, bench, length, shard, half_width, features, columns, layers = shapes
    n_dp, n_tensor, n_layer = sizes
    return (
        n_tensor == 2 and n_layer == 2 and layers == 1 and half_width == 64 and length == 16
        and bench == 16 and train == 32 and n_dp == 4
        and shard % 256 == 0 and columns % 128 == 0 and features == 4096
        and features == 2 * n_dp * columns
    )


def local_any(*args):
    train_inputs, _, bench_inputs, _, _, factors, precond = args
    shapes = (
        train_inputs.shape[1], bench_inputs.shape[1], train_inputs.shape[2], train_inputs.shape[3],
        factors.shape[2] // 2, precond.shape[1], precond.shape[2], train_inputs.shape[0],
    )
    sizes = tuple(lax.axis_size(name) for name in ("dp", "tensor", "layer"))
    return fused(*args) if fits(shapes, sizes) else local(*args)


def solution(mesh):
    placed = (
        P("layer", ("groups", "dp"), None, "tensor"),
        P("layer", ("groups", "dp"), None, "tensor"),
        P("layer", ("groups", "dp"), None, "tensor"),
        P("layer", ("groups", "dp"), None, "tensor"),
        P(("groups", "dp"), None),
        P("layer", "tensor", None),
        P("layer", None, ("dp", "tensor")),
    )
    return jax.shard_map(
        local_any,
        mesh=mesh,
        in_specs=placed,
        out_specs=P(("groups", "dp", "tensor", "layer"), None),
        check_vma=False,
    )
```

```python
import functools
import math

import jax
import jax.numpy as jnp
from jax import lax
from jax.experimental import pallas as pl
from jax.experimental.pallas import tpu as pltpu
from jax.sharding import PartitionSpec as P

MESH = pl.DeviceIdType.MESH


def project(inputs_here, grads_here, factor):
    examples, length, shard_width = inputs_here.shape
    factor_width = factor.shape[1] // 2
    in_proj = jnp.dot(
        inputs_here.reshape(examples * length, shard_width),
        factor[:, :factor_width],
        preferred_element_type=jnp.float32,
    )
    out_proj = jnp.dot(
        grads_here.reshape(examples * length, shard_width),
        factor[:, factor_width:],
        preferred_element_type=jnp.float32,
    )
    return jnp.concatenate([in_proj, out_proj], axis=1)


def outer_features(token_rows, examples, length, factor_width):
    grouped = token_rows.reshape(examples, length, 2 * factor_width)
    outer = jnp.einsum(
        "esa,esb->eab",
        grouped[..., factor_width:],
        grouped[..., :factor_width],
        precision=lax.Precision.HIGHEST,
    ) / math.sqrt(length)
    return outer.reshape(examples, factor_width * factor_width).astype(jnp.bfloat16)


def local(train_inputs, train_grads, bench_inputs, bench_grads, answer_mask, factors, precond):
    factor = factors[0]
    factor_width = factor.shape[1] // 2
    length = train_inputs.shape[2]
    masked = bench_grads[0] * answer_mask.astype(jnp.bfloat16)[:, :, None]
    train_rows = project(train_inputs[0], train_grads[0], factor)
    bench_rows = project(bench_inputs[0], masked, factor)
    tensor_count = lax.axis_size("tensor")
    train_each = train_inputs.shape[1] // tensor_count
    bench_each = bench_inputs.shape[1] // tensor_count
    row_width = train_rows.shape[1]
    blocks = jnp.concatenate(
        [
            train_rows.reshape(tensor_count, train_each * length, row_width),
            bench_rows.reshape(tensor_count, bench_each * length, row_width),
        ],
        axis=1,
    ).reshape(-1, row_width)
    share_rows = blocks.shape[0] // tensor_count
    summed = lax.psum(blocks, "tensor")
    own_rows = lax.dynamic_slice_in_dim(
        summed, lax.axis_index("tensor") * share_rows, share_rows, 0
    )
    train_feats = outer_features(own_rows[: train_each * length], train_each, length, factor_width)
    bench_feats = outer_features(own_rows[train_each * length :], bench_each, length, factor_width)
    columns = precond[0]
    pre_cols = jnp.dot(
        lax.all_gather(bench_feats, ("dp", "tensor"), axis=0, tiled=True),
        columns,
        preferred_element_type=jnp.float32,
    ).astype(jnp.bfloat16)
    layer_total = lax.axis_size("layer") * train_inputs.shape[0]
    score_scale = 1.0 / math.sqrt(factor_width * factor_width * layer_total)
    whole_pre = lax.all_gather(pre_cols, ("dp", "tensor"), axis=1, tiled=True)
    partial_value = jnp.einsum(
        "ek,jk->ej", train_feats, whole_pre, preferred_element_type=jnp.float32
    )
    scores = lax.psum_scatter(partial_value, "layer", scatter_dimension=0, tiled=True)
    return scores * score_scale


def fused_kernel(
    dims,
    ti, tg, bi, bg, mask, fac, pre,
    out,
    bench_v, train_v, fac_v, mask_v, pre_v,
    bench_part, bench_send, bench_recv, train_part, train_recv,
    proj, feats, t_send, t_all, partial_v, score_recv,
    load_sem, swap_recv, gather_recv, t_recv, score_sem, send_sem,
):
    n_dp, scale = dims
    f32, bf16 = jnp.float32, jnp.bfloat16
    z, x, layer = lax.axis_index("dp"), lax.axis_index("tensor"), lax.axis_index("layer")
    other = 1 - x
    me = z * 2 + x
    slots = 2 * n_dp
    length = mask.shape[1]
    shard = fac.shape[0]
    columns = pre_v.shape[1]
    width = 64
    tile = 8 * length
    piece = tile // 2
    along = (((1,), (1,)), ((), ()))

    def load(source, target, index):
        copy = pltpu.make_async_copy(source, target, load_sem.at[index])
        copy.start()
        return copy

    def rows_of(ref, index, rows):
        return ref.at[pl.ds(pl.multiple_of(index * rows, rows), rows), :]

    mask_load = load(mask, mask_v, 0)
    fac_load = load(fac, fac_v, 1)
    for q in range(4):
        for i, ref in enumerate((bi, bg)):
            load(rows_of(ref, q, piece), bench_v.at[q, i], 2 + q)
    for b, index in enumerate((2 * other, 2 * other + 1, 2 * x, 2 * x + 1)):
        for i, ref in enumerate((ti, tg)):
            load(rows_of(ref, index, tile), train_v.at[b, i], 6 + min(b, 2))
    pre_load = load(pre, pre_v, 9)

    def landed(ref, sem):
        pltpu.make_async_copy(ref, ref, sem).wait()

    near = jnp.where(2 * z < n_dp, z, n_dp - 1 - z)

    def line(i):
        place = jnp.where(near <= i, i + 1, i)
        return jnp.where(2 * z < n_dp, place, n_dp - 1 - place)

    others = [line(i) for i in range(n_dp - 1)]

    stage = jnp.where(z > 1, 0, jnp.where(z + x > 0, 1, 2))

    barrier = pltpu.get_barrier_semaphore()
    for where in [{"dp": one} for one in others] + [{"tensor": other}, {"layer": 1 - layer}]:
        pl.semaphore_signal(barrier, inc=1, device_id=where, device_id_type=MESH)

    def remote(source, target, send, recv, where):
        return pltpu.make_async_remote_copy(
            source, target, send, recv, device_id=where, device_id_type=MESH
        )

    lane8 = lax.broadcasted_iota(jnp.int32, (8, tile), 1)
    row8 = lax.broadcasted_iota(jnp.int32, (8, tile), 0)
    root = 1.0 / math.sqrt(length)
    train_block = jnp.where(lane8 // length == row8, root, 0.0)
    bench_block = jnp.where((lane8 // length + 4) % 8 == row8, root, 0.0)

    def project(ref):
        rows = ref.shape[1]
        both = jnp.dot(
            ref[...].reshape(2 * rows, shard), fac_v[...], preferred_element_type=f32
        )
        lane = lax.broadcasted_iota(jnp.int32, (rows, 128), 1)
        return jnp.where(lane < width, both[:rows], both[rows:])

    def spread(rows, block):
        whole = jnp.broadcast_to(rows[:, None, :], (width, 8, tile)) * block[None]
        pairs = whole.reshape(width // 2, 2, 8, tile)
        even = pairs[:, 0].reshape(width * 4, tile)
        odd = pairs[:, 1].reshape(width * 4, tile)
        return jnp.concatenate([even, odd], axis=1)

    def paired(rows):
        zero = jnp.zeros_like(rows)
        return jnp.concatenate(
            [jnp.concatenate([rows, zero], axis=1), jnp.concatenate([zero, rows], axis=1)], axis=0
        )

    def outer(left, right):
        return lax.dot_general(left, right, along, preferred_element_type=f32).reshape(
            width // 2, 8, 128
        )

    def bench_outer(first, second):
        first, second = first[...].astype(f32), second[...].astype(f32)
        lane = lax.broadcasted_iota(jnp.int32, first.shape, 1)
        ins = jnp.where(lane < width, second, pltpu.roll(first, width, 1))
        outs = jnp.where(lane < width, pltpu.roll(second, width, 1), first)
        return outer(spread(outs, bench_block).astype(bf16), paired(ins).astype(bf16))

    def train_outer(whole):
        left, right = spread(whole[width:], train_block), paired(whole[:width])
        left_high, right_high = left.astype(bf16), right.astype(bf16)
        left_low = (left - left_high.astype(f32)).astype(bf16)
        right_low = (right - right_high.astype(f32)).astype(bf16)
        return outer(
            jnp.concatenate([left_high, left_low, left_high], axis=1),
            jnp.concatenate([right_high, right_high, right_low], axis=1),
        )

    with jax.named_scope("keep"):
        mask_load.wait()
        keeps = []
        lay = jnp.where(
            lax.broadcasted_iota(jnp.int32, (length, tile), 1) % length
            == lax.broadcasted_iota(jnp.int32, (length, tile), 0),
            1.0, 0.0,
        ).astype(bf16)
        for q in range(4):
            flags = mask_v[pl.ds(q // 2 * 8, 8), :].astype(f32).astype(bf16)
            tiled = jnp.dot(flags, lay, preferred_element_type=f32)
            wanted = (lane8 >= width) & ((lane8 - width) // length + 4 * (q % 2) == row8)
            masked = jnp.where(wanted, tiled, jnp.where((lane8 < width) & (row8 == 0), 1.0, 0.0))
            keeps.append(
                jnp.dot(jnp.ones((width, 8), bf16), masked.astype(bf16), preferred_element_type=f32)
            )

    bench_swaps = [
        remote(
            bench_send.at[q], bench_recv.at[q], send_sem.at[0], swap_recv.at[q], {"tensor": other}
        )
        for q in range(4)
    ]
    train_swaps = [
        remote(
            train_part.at[b], train_recv.at[b], send_sem.at[0], swap_recv.at[4 + b],
            {"tensor": other},
        )
        for b in range(2)
    ]

    with jax.named_scope("fac_wait"):
        fac_load.wait()
    for q in range(4):
        with jax.named_scope("bench_load_wait"):
            landed(bench_v.at[q], load_sem.at[2 + q])
        with jax.named_scope("bench_project"):
            value = project(bench_v.at[q])
            bench_part[q] = value
            bench_send[q] = value.astype(bf16)

        @pl.when(stage == 0)
        def _(q=q):
            if q == 0:
                pl.semaphore_wait(barrier, n_dp + 1)
            bench_swaps[q].start()

    @pl.when(stage == 1)
    def _():
        pl.semaphore_wait(barrier, n_dp + 1)
        for one in bench_swaps:
            one.start()

    def train_project(b):
        with jax.named_scope("train_load_wait"):
            if b < 2:
                landed(train_v.at[b], load_sem.at[6 + b])
            elif b == 2:
                landed(train_v.at[pl.ds(2, 2)], load_sem.at[8])
        with jax.named_scope("train_project"):
            train_part[b] = project(train_v.at[b])

    for b in range(2):
        train_project(b)

        @pl.when((stage < 2) & (layer == 0))
        def _(b=b):
            train_swaps[b].start()

    @pl.when(stage == 2)
    def _():
        pl.semaphore_wait(barrier, n_dp + 1)
        for one in bench_swaps:
            one.start()

    @pl.when((stage == 2) & (layer == 0))
    def _():
        for one in train_swaps:
            one.start()

    @pl.when(stage == 2)
    def _():
        for b in range(2):
            train_project(2 + b)

    for q in range(4):
        with jax.named_scope("bench_swap_wait"):
            bench_swaps[q].wait_recv()
        with jax.named_scope("bench_turn"):
            turned = (bench_part[q] + bench_recv[q].astype(f32)).T
            proj[z, q] = (
                jnp.concatenate([turned[:width], turned[width:]], axis=1) * keeps[q]
            ).astype(bf16)

        def gather(q, one):
            remote(
                proj.at[z, q], proj.at[z, q], send_sem.at[0], gather_recv.at[z], {"dp": one}
            ).start()

        @pl.when((layer == 0) | (x == q // 2))
        def _(q=q):
            for one in others[:0:-1]:
                gather(q, one)

        gather(q, others[0])

    @pl.when(layer == 1)
    def _():
        for one in train_swaps:
            one.start()

    @pl.when(stage < 2)
    def _():
        for b in range(2):
            train_project(2 + b)

    def bench_feats(slot):
        with jax.named_scope("bench_feats"):
            both = jnp.concatenate(
                [bench_outer(proj.at[slot, 2 * h], proj.at[slot, 2 * h + 1]) for h in range(2)],
                axis=1,
            ).astype(bf16)
            for p in range(width // 2):
                feats[slot, :, p * 128 : p * 128 + 128] = both[p]

    order = [others[0]] + others[:0:-1]

    passed = [z, n_dp]

    def forward():
        for index, slot in enumerate(order[1:]):
            half = proj.at[slot, pl.ds(2 * x, 2)]
            landed(half, gather_recv.at[slot])
            remote(half, half, send_sem.at[0], gather_recv.at[passed[index]], {"tensor": other}).start()

    pl.when((layer == 1) & (z > 0))(forward)

    halves = []
    for b in range(2):
        with jax.named_scope("train_swap_wait"):
            train_swaps[b].wait_recv()
        with jax.named_scope("train_feats"):
            halves.append(train_outer((train_part[2 + b] + train_recv[b]).T))
    with jax.named_scope("train_store"):
        both = jnp.concatenate(halves, axis=1).astype(bf16)
        per_slot = columns // 128
        for p in range(width // 2):
            at = p % per_slot * 128
            t_send[p // per_slot, :, at : at + 128] = both[p]

    def t_copy(target, where):
        remote(t_send.at[target], t_all.at[me], send_sem.at[1], t_recv.at[z], where).start()

    for one in reversed(others):
        for column in range(2):
            t_copy(one * 2 + column, {"dp": one, "tensor": column})
    t_copy(z * 2 + other, {"tensor": other})
    pltpu.make_async_copy(t_send.at[me], t_all.at[me], t_recv.at[z]).start()
    pl.when((layer == 1) & (z == 0))(forward)
    bench_feats(z)

    for place, slot in enumerate(order):
        with jax.named_scope("gather_wait"):

            if place == 0:
                landed(proj.at[slot], gather_recv.at[slot])
            else:

                @pl.when(layer == 0)
                def _(slot=slot):
                    landed(proj.at[slot], gather_recv.at[slot])

                @pl.when(layer == 1)
                def _(slot=slot, place=place):
                    landed(proj.at[slot, pl.ds(0, 2)], gather_recv.at[passed[place - 1]])

        bench_feats(slot)

    with jax.named_scope("pre_wait"):
        pre_load.wait()
    with jax.named_scope("pre_dot"):
        bench_pre = jnp.dot(
            feats[...].reshape(n_dp * 16, feats.shape[2]), pre_v[...], preferred_element_type=f32
        )
        pre_high = bench_pre.astype(bf16)
        pre_low = (bench_pre - pre_high.astype(f32)).astype(bf16)
        pre_both = jnp.concatenate([pre_high, pre_low], axis=0)

    own = me * 2 + layer
    low_lanes = lax.broadcasted_iota(jnp.int32, (32, 128), 1) < width
    half_rows = pl.ds(0, 4)
    landing = score_recv.at[own, half_rows]
    for at in range(n_dp):
        with jax.named_scope("t_wait"):
            landed(t_all.at[pl.ds(2 * at, 2)], t_recv.at[at])
        with jax.named_scope("score_dot"):
            held = t_all[2 * at : 2 * at + 2].reshape(32, columns)
            wide = lax.dot_general(held, pre_both, along, preferred_element_type=f32)
            both = wide + pltpu.roll(wide, n_dp * 16, 1)
            packed = jnp.where(low_lanes, both, pltpu.roll(both, 28, 0))
            partial_v[4 * at : 4 * at + 4] = packed.reshape(4, 8, 128)
        for column, core in ((other, 1 - layer), (other, layer), (x, 1 - layer)):
            remote(
                partial_v.at[4 * at + 2 * column + core, half_rows], landing,
                send_sem.at[2], score_sem.at[0],
                {"dp": at, "tensor": column, "layer": core},
            ).start()
        mine = partial_v.at[4 * at + 2 * x + layer, half_rows]

        @pl.when(z == at)
        def _():
            pltpu.make_async_copy(mine, landing, score_sem.at[0]).start()

        @pl.when(z != at)
        def _():
            remote(mine, landing, send_sem.at[2], score_sem.at[0], {"dp": at}).start()

    with jax.named_scope("score_wait"):
        landed(score_recv.at[pl.ds(0, slots)], score_sem.at[0])
    result = score_recv[0, :4, :]
    for index in range(1, 2 * slots):
        result = result + score_recv[index, :4, :]
    result = result * scale
    out[:4, :] = result[:, :width]
    out[4:, :] = result[:, width:]

    with jax.named_scope("send_wait"):
        landed(train_v.at[0, 0, pl.ds(0, 3 * tile // 8)], send_sem.at[0])
        landed(t_send.at[pl.ds(0, slots - 1)], send_sem.at[1])
        landed(partial_v.at[pl.ds(0, 2 * slots - 1), half_rows], send_sem.at[2])


def fused(train_inputs, train_grads, bench_inputs, bench_grads, answer_mask, factors, precond):
    f32, bf16 = jnp.float32, jnp.bfloat16
    _, train, length, shard = train_inputs.shape
    bench = bench_inputs.shape[1]
    n_dp = lax.axis_size("dp")
    slots = 2 * n_dp
    features, columns = precond.shape[1:]
    scale = 1.0 / math.sqrt(features * lax.axis_size("layer"))
    tile = 8 * length
    dma = pltpu.SemaphoreType.DMA
    anywhere = pl.BlockSpec(memory_space=pl.ANY)
    return pl.pallas_call(
        functools.partial(fused_kernel, (n_dp, scale)),
        out_shape=pltpu.VMEM((8, n_dp * bench), f32),
        in_specs=[anywhere] * 7,
        out_specs=pl.BlockSpec(memory_space=pltpu.VMEM),
        scratch_shapes=[
            pltpu.VMEM((4, 2, tile // 2, shard), bf16),
            pltpu.VMEM((4, 2, tile, shard), bf16),
            pltpu.VMEM((shard, 128), bf16),
            pltpu.VMEM((bench, length), jnp.int32),
            pltpu.VMEM((features, columns), bf16),
            pltpu.VMEM((4, tile // 2, 128), f32),
            pltpu.VMEM((4, tile // 2, 128), bf16),
            pltpu.VMEM((4, tile // 2, 128), bf16),
            pltpu.VMEM((4, tile, 128), f32),
            pltpu.VMEM((2, tile, 128), f32),
            pltpu.VMEM((n_dp, 4, 64, 128), bf16),
            pltpu.VMEM((n_dp, bench, features), bf16),
            pltpu.VMEM((slots, 16, columns), bf16),
            pltpu.VMEM((slots, 16, columns), bf16),
            pltpu.VMEM((2 * slots, 8, 128), f32),
            pltpu.VMEM((2 * slots, 8, 128), f32),
            dma((10,)),
            dma((6,)),
            dma((n_dp + 1,)),
            dma((n_dp,)),
            dma((1,)),
            dma((3,)),
        ],
        compiler_params=pltpu.CompilerParams(
            collective_id=0, has_side_effects=True, vmem_limit_bytes=56 * 1024 * 1024
        ),
    )(
        train_inputs.reshape(train * length, shard),
        train_grads.reshape(train * length, shard),
        bench_inputs.reshape(bench * length, shard),
        bench_grads.reshape(bench * length, shard),
        answer_mask,
        factors[0],
        precond[0],
    )


def fits(shapes, sizes):
    train, bench, length, shard, half_width, features, columns, layers = shapes
    n_dp, n_tensor, n_layer = sizes
    return (
        n_tensor == 2 and n_layer == 2 and layers == 1 and half_width == 64 and length == 16
        and bench == 16 and train == 32 and n_dp == 4
        and shard % 256 == 0 and columns % 128 == 0 and features == 4096
        and features == 2 * n_dp * columns
    )


def local_any(*args):
    train_inputs, _, bench_inputs, _, _, factors, precond = args
    shapes = (
        train_inputs.shape[1], bench_inputs.shape[1], train_inputs.shape[2], train_inputs.shape[3],
        factors.shape[2] // 2, precond.shape[1], precond.shape[2], train_inputs.shape[0],
    )
    sizes = tuple(lax.axis_size(name) for name in ("dp", "tensor", "layer"))
    return fused(*args) if fits(shapes, sizes) else local(*args)


def solution(mesh):
    placed = (
        P("layer", ("groups", "dp"), None, "tensor"),
        P("layer", ("groups", "dp"), None, "tensor"),
        P("layer", ("groups", "dp"), None, "tensor"),
        P("layer", ("groups", "dp"), None, "tensor"),
        P(("groups", "dp"), None),
        P("layer", "tensor", None),
        P("layer", None, ("dp", "tensor")),
    )
    return jax.shard_map(
        local_any,
        mesh=mesh,
        in_specs=placed,
        out_specs=P(("groups", "dp", "tensor", "layer"), None),
        check_vma=False,
    )
```
